512 devices in a mesh: gx: 16 (over z, y_lo), gy: 16 (over y_hi, x), comp: 2 (over core).
Axes of the slice: x: 4, y: 8 (y_hi: 4, y_lo: 2; y = y_hi * 2 + y_lo), z: 8, core: 2. Of those that a mesh axis runs over, the one named last changes fastest.
Arguments:
- spectrum: bfloat16 [256, 2048, 1024], P('gx', 'gy', 'comp'), may hold values from -6 to 6
- sea_mask: int32 [256, 2048], P('gx', 'gy'), may hold values 0 or 1
- courant: float32 [2, 1024], P(None, 'comp'), may hold values from -0.45 to 0.45
- interaction: bfloat16 [1024, 1024], replicated, may hold values from -0.1875 to 0.1875
- stokes_proj: bfloat16 [2, 1024, 64], replicated, may hold values from -0.1875 to 0.1875
- currents: float32 [2, 64, 256, 2048], P(None, 'comp', 'gx', 'gy'), may hold values from -6 to 6
- level_drag: float32 [64], P('comp'), may hold values from 0.05 to 0.5
Outputs:
- wave_out: bfloat16 [256, 2048, 1024], P('gx', 'gy', 'comp')
- currents_out: float32 [2, 64, 256, 2048], P(None, 'comp', 'gx', 'gy')
The draws below stay inside these ranges and needn't reach their ends.
All inputs are finite; a program needn't handle non-finite values. No bound on the sum of `sea_mask` on one device may be relied on, other than what follows from the above.
Results may differ from the reference program's by a relative error of at most 0.0049.
Values may be sent and summed in bfloat16 or wider, within the bound.
A program may use at most 64 MiB of HBM per device.

```python
import math
import jax
import jax.numpy as jnp
from jax import lax

K = 1024
LEV = 64
SUBSTEPS = 3
NX = 256
NY = 2048


def plant(drawn, rng, low, top_value):
    longest = drawn.shape.index(max(drawn.shape))
    spots = []
    for shift in (0, 1):
        where = [jax.random.randint(jax.random.fold_in(rng, axis), (), 0, length) for axis, length in enumerate(drawn.shape)]
        where[longest] = (where[longest] + shift) % drawn.shape[longest]
        spots.append(tuple(where))
    return drawn.at[spots[0]].set(low).at[spots[1]].set(top_value)


def steps_of(stream_key, shape, pieces, least, high):
    loudness = 1.0
    for position, shards_of in pieces:
        heights = jax.random.uniform(jax.random.fold_in(jax.random.fold_in(stream_key, 6), position), (shards_of,), jnp.float32, least / len(pieces), high / len(pieces))
        loudness = loudness * jnp.repeat(jnp.exp(heights), shape[position] // shards_of).reshape((-1,) + (1,) * (len(shape) - 1 - position))
    return loudness


def noise(own_key, shape, deviation, most, pieces=(), kind=jnp.bfloat16):
    level = steps_of(own_key, shape, pieces, -0.22, 0.18) if pieces else 1.0
    result = jax.random.normal(own_key, shape, jnp.float32) * deviation * level
    return jnp.minimum(jnp.maximum(result, -most), most).astype(kind)


def setup_inputs(seed: int = 0) -> dict:
    key_of = jax.random.split(jax.random.key(seed), 8)
    return {
        "spectrum": noise(key_of[0], (NX, NY, K), 1.0, 6.0, ((0, 16), (1, 16), (2, 2))),
        "sea_mask": plant((jax.random.randint(key_of[1], (NX, NY), 0, 4) < 3).astype(jnp.int32), jax.random.fold_in(key_of[1], 1), 0, 1),
        "courant": jnp.clip(jax.random.uniform(key_of[2], (2, K), jnp.float32, -0.45, 0.45) * steps_of(key_of[2], (2, K), ((1, 2),), -0.4, 0.0), -0.45, 0.45),
        "interaction": noise(key_of[3], (K, K), K ** -0.5, 0.1875),
        "stokes_proj": noise(key_of[4], (2, K, LEV), K ** -0.5, 0.1875),
        "currents": noise(key_of[5], (2, LEV, NX, NY), 1.0, 6.0, ((1, 2), (2, 16), (3, 16)), jnp.float32),
        "level_drag": jnp.clip(jnp.exp(math.log(0.5) - 2.3025851 * jax.random.uniform(key_of[6], (LEV,), jnp.float32) ** steps_of(key_of[6], (LEV,), ((0, 2),), -0.2, 0.2)), 0.05, 0.5),
    }


time_step = 0.5
viscosity = 0.4


def upwind(centre, west_cell, east_cell, south_cell, north_cell, courant):
    cour_x = courant[0]
    cour_y = courant[1]
    return (centre - jnp.maximum(cour_x, 0.0) * (centre - west_cell)
            - jnp.minimum(cour_x, 0.0) * (east_cell - centre)
            - jnp.maximum(cour_y, 0.0) * (centre - south_cell)
            - jnp.minimum(cour_y, 0.0) * (north_cell - centre))


def substep(u_pad, v_pad, stokes_u, stokes_v, coriolis, sea_cells, level_drag):
    u_mid = u_pad[:, 1:-1, 1:-1]
    v_mid = v_pad[:, 1:-1, 1:-1]
    vorticity = 0.5 * (v_pad[:, 2:, 1:-1] - v_pad[:, :-2, 1:-1]) - 0.5 * (u_pad[:, 1:-1, 2:] - u_pad[:, 1:-1, :-2])
    lap_u = u_pad[:, 2:, 1:-1] + u_pad[:, :-2, 1:-1] + u_pad[:, 1:-1, 2:] + u_pad[:, 1:-1, :-2] - 4.0 * u_mid
    lap_v = v_pad[:, 2:, 1:-1] + v_pad[:, :-2, 1:-1] + v_pad[:, 1:-1, 2:] + v_pad[:, 1:-1, :-2] - 4.0 * v_mid
    abs_vort = coriolis + vorticity
    drag_col = level_drag[:, None, None]
    u_next = u_mid + time_step * (abs_vort * (v_mid + stokes_v) - drag_col * u_mid + viscosity * lap_u)
    v_next = v_mid + time_step * (-abs_vort * (u_mid + stokes_u) - drag_col * v_mid + viscosity * lap_v)
    return u_next * sea_cells, v_next * sea_cells


def pad_field(field):
    wrapped = jnp.concatenate([field[:, -1:], field, field[:, :1]], axis=1)
    return jnp.pad(wrapped, ((0, 0), (0, 0), (1, 1)))


def reference(spectrum, sea_mask, courant, interaction, stokes_proj, currents, level_drag):
    sea_cells = sea_mask.astype(jnp.float32)
    proj_wide = stokes_proj.astype(jnp.float32)

    def row_work(row_index):
        row_index = row_index.astype(jnp.int32)
        centre = lax.dynamic_index_in_dim(spectrum, row_index, 0, keepdims=False).astype(jnp.float32)
        west_cell = lax.dynamic_index_in_dim(spectrum, (row_index - 1) % NX, 0, keepdims=False).astype(jnp.float32)
        east_cell = lax.dynamic_index_in_dim(spectrum, (row_index + 1) % NX, 0, keepdims=False).astype(jnp.float32)
        south_cell = jnp.pad(centre, ((1, 0), (0, 0)))[:-1]
        north_cell = jnp.pad(centre, ((0, 1), (0, 0)))[1:]
        sea_col = lax.dynamic_index_in_dim(sea_cells, row_index, 0, keepdims=False)[:, None]
        advected = (upwind(centre, west_cell, east_cell, south_cell, north_cell, courant) * sea_col).astype(jnp.bfloat16)
        gain = jnp.dot(advected, interaction, preferred_element_type=jnp.float32)
        wave_row = ((advected.astype(jnp.float32) + gain) * sea_col).astype(jnp.bfloat16)
        stokes_row = jnp.einsum("yk,ckl->cly", advected.astype(jnp.float32), proj_wide)
        return wave_row, stokes_row

    wave_out, stokes_rows = lax.map(row_work, jnp.arange(NX, dtype=jnp.int32))
    stokes = jnp.transpose(stokes_rows, (1, 2, 0, 3))
    lat_index = jnp.arange(NY).astype(jnp.float32)
    coriolis = jnp.sin(jnp.pi * ((lat_index + 0.5) / NY - 0.5))[None, :]
    u_field = currents[0]
    v_field = currents[1]
    for sub_index in range(SUBSTEPS):
        u_field, v_field = substep(pad_field(u_field), pad_field(v_field), stokes[0], stokes[1], coriolis, sea_cells, level_drag)
    return wave_out, jnp.stack([u_field, v_field])
```

```python
import functools

import jax
import jax.numpy as jnp
from jax import lax
from jax.experimental import pallas as pl
from jax.experimental.pallas import tpu as pltpu
from jax.sharding import PartitionSpec as P

SUBSTEPS = 3
DT = 0.5
VISC = 0.4
F32 = jnp.float32
BF16 = jnp.bfloat16
MESH = pl.DeviceIdType.MESH


def kernel(
    dims,
    spec_hbm, mask_hbm, cour_hbm, inter_hbm, proj_hbm, cur_hbm, drag_hbm, cor_hbm,
    wave_hbm, curo_hbm,
    specx, adv, wmat, proj, maskv, cour, curv, dragv, corv,
    maskf, mask_b, fbuf, ystage, ysend, yrecv, yhalo,
    flow, stokes, vsend, vrecv, obuf, coutv,
    load_sem, hx_send, hx_recv, hy_send, hy_recv, av_send, av_recv,
    fx_send, fx_recv, fy_send, fy_recv, out_sem,
):
    nx, ny, nk, nl = dims
    gx, gy, core = lax.axis_index("gx"), lax.axis_index("gy"), lax.axis_index("comp")
    n_gx, n_gy = lax.axis_size("gx"), lax.axis_size("gy")
    west = (lax.rem(gx + n_gx - 1, n_gx), gy, core)
    east = (lax.rem(gx + 1, n_gx), gy, core)
    south = (gx, lax.rem(gy + n_gy - 1, n_gy), core)
    north = (gx, lax.rem(gy + 1, n_gy), core)
    other = 1 - core
    partner = (gx, gy, other)
    not_first = jnp.where(gy > 0, 1.0, 0.0).astype(F32)
    not_last = jnp.where(gy < n_gy - 1, 1.0, 0.0).astype(F32)

    def rows(start, count):
        return pl.ds(pl.multiple_of(start * ny, ny), count * ny)

    loads = []

    def load(src, dst):
        copy = pltpu.make_async_copy(src, dst, load_sem.at[len(loads)])
        copy.start()
        loads.append(copy)
        return copy

    spec_load = load(spec_hbm, specx.at[pl.ds(ny, nx * ny), :])
    mask_load = load(mask_hbm, maskv)
    cour_load = load(cour_hbm, cour)
    cur_load = load(cur_hbm, curv)
    own_k = pl.ds(pl.multiple_of(core * nk, nk), nk)
    oth_k = pl.ds(pl.multiple_of(other * nk, nk), nk)
    own_l = pl.ds(pl.multiple_of(core * nl, nl), nl)
    late = [
        load(drag_hbm, dragv),
        load(cor_hbm, corv),
        load(proj_hbm.at[0, own_l, own_k], proj.at[pl.ds(0, nl), pl.ds(0, nk)]),
        load(proj_hbm.at[0, own_l, oth_k], proj.at[pl.ds(0, nl), pl.ds(nk, nk)]),
        load(proj_hbm.at[1, own_l, own_k], proj.at[pl.ds(nl, nl), pl.ds(0, nk)]),
        load(proj_hbm.at[1, own_l, oth_k], proj.at[pl.ds(nl, nl), pl.ds(nk, nk)]),
        load(inter_hbm.at[own_k, own_k], wmat.at[pl.ds(0, nk), :]),
        load(inter_hbm.at[oth_k, own_k], wmat.at[pl.ds(nk, nk), :]),
    ]

    barrier = pltpu.get_barrier_semaphore()
    for peer in (west, east, south, north, partner):
        pl.semaphore_signal(barrier, inc=1, device_id=peer, device_id_type=MESH)

    def remote(src, dst, send, recv, peer):
        return pltpu.make_async_remote_copy(
            src_ref=src, dst_ref=dst, send_sem=send, recv_sem=recv,
            device_id=peer, device_id_type=MESH,
        )

    spec_load.wait()
    for x in range(nx):
        first = (1 + x) * ny
        ystage[0, x:x + 1, :] = specx[first:first + 16, :].astype(F32)[0:1]
        ystage[1, x:x + 1, :] = specx[first + ny - 16:first + ny, :].astype(F32)[15:16]
    ysend[...] = ystage[...].astype(BF16)

    pl.semaphore_wait(barrier, 5)
    hy = [
        remote(ysend.at[0], yrecv.at[1], hy_send.at[0], hy_recv.at[1], south),
        remote(ysend.at[1], yrecv.at[0], hy_send.at[1], hy_recv.at[0], north),
    ]
    hx = [
        remote(spec_hbm.at[rows(0, 1), :], specx.at[rows(nx + 1, 1), :], hx_send.at[0], hx_recv.at[1], west),
        remote(spec_hbm.at[rows(nx - 1, 1), :], specx.at[rows(0, 1), :], hx_send.at[1], hx_recv.at[0], east),
    ]
    for copy in hy + hx:
        copy.start()

    lane = lax.broadcasted_iota(jnp.int32, (nl, ny), 1)

    def pack(x, u, v, low, high):
        for c, q in ((0, u), (1, v)):
            spot = c * nx + x
            low = jnp.where(lane == spot, pltpu.roll(q, spot, 1), low)
            high = jnp.where(lane == spot, pltpu.roll(q, spot + 1, 1), high)
        return low, high

    def send_flow(s, low, high):
        vsend[s, 0] = low
        vsend[s, 1] = high
        copies = [
            remote(flow.at[s, 1], flow.at[s, nx + 1], fx_send.at[s, 0], fx_recv.at[s, 1], west),
            remote(flow.at[s, nx], flow.at[s, 0], fx_send.at[s, 1], fx_recv.at[s, 0], east),
            remote(vsend.at[s, 0], vrecv.at[s, 1], fy_send.at[s, 0], fy_recv.at[s, 1], south),
            remote(vsend.at[s, 1], vrecv.at[s, 0], fy_send.at[s, 1], fy_recv.at[s, 0], north),
        ]
        for copy in copies:
            copy.start()
        return copies

    zero = jnp.zeros((nl, ny), F32)
    cur_load.wait()

    def first_flow(x, carry):
        u = curv[pl.ds(x, nl, stride=nx), :]
        v = curv[pl.ds(nl * nx + x, nl, stride=nx), :]
        flow[0, x + 1, 0:nl, :] = u
        flow[0, x + 1, nl:2 * nl, :] = v
        return pack(x, u, v, *carry)

    sent = [send_flow(0, *lax.fori_loop(0, nx, first_flow, (zero, zero)))]

    mask_load.wait()
    cour_load.wait()
    own_mask = maskv[...].astype(F32)
    maskf[...] = own_mask
    turned = jnp.concatenate([own_mask, jnp.zeros((ny - nx, ny), F32)], axis=0).T
    for x in range(nx):
        mask_b[x * ny:(x + 1) * ny, :] = jnp.broadcast_to(turned[:, x:x + 1], (ny, 128))

    chunks = nk // 128
    for copy in hy:
        copy.wait_recv()
    for kc in range(chunks):
        ks = slice(kc * 128, (kc + 1) * 128)
        yhalo[0, kc] = yrecv[0, :, ks].astype(F32) * not_first
        yhalo[1, kc] = yrecv[1, :, ks].astype(F32) * not_last

    def advect(x, carry):
        mb = mask_b[rows(x, 1), :]
        for kc in range(chunks):
            ks = slice(kc * 128, (kc + 1) * 128)
            a, b = cour[0:1, ks], cour[1:2, ks]
            mag_a, mag_b = jnp.abs(a), jnp.abs(b)
            here = specx[rows(x + 1, 1), ks].astype(F32)
            fbuf[kc, 8:8 + ny, :] = here
            fbuf[kc, 7:8, :] = yhalo[0, kc, pl.ds(x, 1), :]
            fbuf[kc, 8 + ny:9 + ny, :] = yhalo[1, kc, pl.ds(x, 1), :]
            ux = jnp.where(a > 0, specx[rows(x, 1), ks].astype(F32), specx[rows(x + 2, 1), ks].astype(F32))
            uy = jnp.where(b > 0, fbuf[kc, 7:7 + ny, :], fbuf[kc, 9:9 + ny, :])
            new = (1.0 - mag_a - mag_b) * here + mag_a * ux + mag_b * uy
            adv[rows(x, 1), ks] = (mb * new).astype(BF16)
        swap(x).start()
        return carry

    def swap(x):
        return remote(
            adv.at[rows(x, 1), pl.ds(0, nk)], adv.at[rows(x, 1), pl.ds(nk, nk)],
            av_send.at[x], av_recv.at[x], partner,
        )

    lax.fori_loop(1, nx - 1, advect, 0)
    for copy in hx:
        copy.wait_recv()
    advect(0, 0)
    advect(nx - 1, 0)

    for copy in late:
        copy.wait()

    def drift(p, carry):
        swap(2 * p).wait_recv()
        swap(2 * p + 1).wait_recv()
        both = lax.dot_general(
            proj[...], adv[rows(2 * p, 2), :], (((1,), (1,)), ((), ())),
            preferred_element_type=F32,
        )
        stokes[2 * p] = both[:, :ny]
        stokes[2 * p + 1] = both[:, ny:]
        return carry

    lax.fori_loop(0, nx // 2, drift, 0)

    eye = lax.broadcasted_iota(jnp.int32, (nl, nl), 0) == lax.broadcasted_iota(jnp.int32, (nl, nl), 1)
    drag = jnp.sum(jnp.where(eye, jnp.broadcast_to(dragv[...], (nl, nl)), 0.0), axis=1, keepdims=True)
    drag = jnp.broadcast_to(drag, (nl, ny))
    cor = corv[...]

    def substep(s):
        for copy in sent[s]:
            copy.wait_recv()
        south_halo = vrecv[s, 0] * not_first
        north_halo = vrecv[s, 1] * not_last

        def sides(x, c, q):
            spot = c * nx + x
            low = jnp.where(lane == 0, pltpu.roll(south_halo, ny - spot, 1), pltpu.roll(q, 1, 1))
            high = jnp.where(lane == ny - 1, pltpu.roll(north_halo, ny - 1 - spot, 1), pltpu.roll(q, ny - 1, 1))
            return low, high

        def step(x, carry):
            lev_u, lev_v = pl.ds(0, nl), pl.ds(nl, nl)
            u, v = flow[s, x + 1, lev_u, :], flow[s, x + 1, lev_v, :]
            u_w, v_w = flow[s, x, lev_u, :], flow[s, x, lev_v, :]
            u_e, v_e = flow[s, x + 2, lev_u, :], flow[s, x + 2, lev_v, :]
            u_s, u_n = sides(x, 0, u)
            v_s, v_n = sides(x, 1, v)
            total = cor + 0.5 * (v_e - v_w) - 0.5 * (u_n - u_s)
            lap_u = u_e + u_w + u_n + u_s - 4.0 * u
            lap_v = v_e + v_w + v_n + v_s - 4.0 * v
            m = maskf[pl.ds(x, 1), :]
            u_new = m * (u + DT * (total * (v + stokes[x, lev_v, :]) - drag * u + VISC * lap_u))
            v_new = m * (v + DT * (-total * (u + stokes[x, lev_u, :]) - drag * v + VISC * lap_v))
            if s == SUBSTEPS - 1:
                coutv[pl.ds(x, nl, stride=nx), :] = u_new
                coutv[pl.ds(nl * nx + x, nl, stride=nx), :] = v_new
                return carry
            flow[s + 1, x + 1, lev_u, :] = u_new
            flow[s + 1, x + 1, lev_v, :] = v_new
            return pack(x, u_new, v_new, *carry)

        if s == SUBSTEPS - 1:
            lax.fori_loop(0, nx, step, 0)
        else:
            sent.append(send_flow(s + 1, *lax.fori_loop(0, nx, step, (zero, zero))))

    group, wide = 4, 256

    def put(g):
        return pltpu.make_async_copy(
            obuf.at[rows(g * group, group), :], wave_hbm.at[rows(g * group, group), :], out_sem.at[g]
        )

    def gain(g, carry):
        rs = rows(g * group, group)
        mb = mask_b[rs, :]
        mb = jnp.concatenate([mb] * (wide // 128), axis=1)
        for n in range(nk // wide):
            ns = slice(n * wide, (n + 1) * wide)
            got = jnp.dot(adv[rs, :], wmat[:, ns], preferred_element_type=F32)
            obuf[rs, ns] = (mb * (adv[rs, ns].astype(F32) + got)).astype(BF16)
        put(g).start()
        return carry

    groups = nx // group
    substep(0)
    lax.fori_loop(0, groups // 2, gain, 0)
    substep(1)
    lax.fori_loop(groups // 2, groups, gain, 0)
    substep(2)
    cout = pltpu.make_async_copy(coutv, curo_hbm, out_sem.at[groups])
    cout.start()

    for copy in hy + hx + [c for copies in sent for c in copies]:
        copy.wait_send()

    def drain(x, carry):
        swap(x).wait_send()
        return carry

    lax.fori_loop(0, nx, drain, 0)

    def drain_out(g, carry):
        put(g).wait()
        return carry

    lax.fori_loop(0, groups, drain_out, 0)
    cout.wait()


def local(spectrum, sea_mask, courant, interaction, stokes_proj, currents, level_drag):
    nx, ny, nk = spectrum.shape
    nl = currents.shape[1]
    ny_total = lax.axis_size("gy") * ny
    lat_index = lax.axis_index("gy") * ny + jnp.arange(ny)
    coriolis = jnp.sin(jnp.pi * ((lat_index.astype(F32) + 0.5) / ny_total - 0.5))[None, :]
    any_space = pl.BlockSpec(memory_space=pl.ANY)
    groups = nx // 4
    dma = pltpu.SemaphoreType.DMA
    wave, cur = pl.pallas_call(
        functools.partial(kernel, (nx, ny, nk, nl)),
        out_shape=(
            jax.ShapeDtypeStruct((nx * ny, nk), BF16),
            jax.ShapeDtypeStruct((2 * nl * nx, ny), F32),
        ),
        in_specs=[any_space] * 8,
        out_specs=(any_space, any_space),
        scratch_shapes=[
            pltpu.VMEM(((nx + 2) * ny, nk), BF16),
            pltpu.VMEM((nx * ny, 2 * nk), BF16),
            pltpu.VMEM((2 * nk, nk), BF16),
            pltpu.VMEM((2 * nl, 2 * nk), BF16),
            pltpu.VMEM((nx, ny), jnp.int32),
            pltpu.VMEM((2, nk), F32),
            pltpu.VMEM((2 * nl * nx, ny), F32),
            pltpu.VMEM((1, nl), F32),
            pltpu.VMEM((1, ny), F32),
            pltpu.VMEM((nx, ny), F32),
            pltpu.VMEM((nx * ny, 128), F32),
            pltpu.VMEM((nk // 128, ny + 16, 128), F32),
            pltpu.VMEM((2, nx, nk), F32),
            pltpu.VMEM((2, nx, nk), BF16),
            pltpu.VMEM((2, nx, nk), BF16),
            pltpu.VMEM((2, nk // 128, nx, 128), F32),
            pltpu.VMEM((SUBSTEPS, nx + 2, 2 * nl, ny), F32),
            pltpu.VMEM((nx, 2 * nl, ny), F32),
            pltpu.VMEM((SUBSTEPS, 2, nl, ny), F32),
            pltpu.VMEM((SUBSTEPS, 2, nl, ny), F32),
            pltpu.VMEM((nx * ny, nk), BF16),
            pltpu.VMEM((2 * nl * nx, ny), F32),
            dma((12,)),
            dma((2,)), dma((2,)), dma((2,)), dma((2,)),
            dma((nx,)), dma((nx,)),
            dma((SUBSTEPS, 2)), dma((SUBSTEPS, 2)), dma((SUBSTEPS, 2)), dma((SUBSTEPS, 2)),
            dma((groups + 1,)),
        ],
        compiler_params=pltpu.CompilerParams(
            collective_id=0, has_side_effects=True, vmem_limit_bytes=48 * 1024 * 1024
        ),
        name="wave_ocean",
    )(
        spectrum.reshape(nx * ny, nk),
        sea_mask,
        courant,
        interaction,
        jnp.transpose(stokes_proj, (0, 2, 1)),
        currents.reshape(2 * nl * nx, ny),
        level_drag[None, :],
        coriolis,
    )
    return wave.reshape(nx, ny, nk), cur.reshape(2, nl, nx, ny)


def solution(mesh):
    in_specs = (
        P("gx", "gy", "comp"),
        P("gx", "gy"),
        P(None, "comp"),
        P(),
        P(),
        P(None, "comp", "gx", "gy"),
        P("comp"),
    )
    out_specs = (P("gx", "gy", "comp"), P(None, "comp", "gx", "gy"))
    return jax.shard_map(local, mesh=mesh, in_specs=in_specs, out_specs=out_specs, check_vma=False)
```

```python
import functools

import jax
import jax.numpy as jnp
from jax import lax
from jax.experimental import pallas as pl
from jax.experimental.pallas import tpu as pltpu
from jax.sharding import PartitionSpec as P

SUBSTEPS = 3
DT = 0.5
VISC = 0.4
F32 = jnp.float32
BF16 = jnp.bfloat16
MESH = pl.DeviceIdType.MESH


def kernel(
    dims,
    spec_hbm, mask_hbm, cour_hbm, inter_hbm, proj_hbm, cur_hbm, drag_hbm, cor_hbm,
    wave_hbm, curo_hbm,
    specx, adv, wmat, proj, maskv, cour, curv, dragv, corv,
    maskf, mask_b, drag_b, fbuf, ystage, ysend, yrecv, yhalo,
    flow, stokes, vsend, vrecv, obuf, coutv,
    load_sem, hx_send, hx_recv, hy_send, hy_recv, av_send, av_recv,
    fx_send, fx_recv, fy_send, fy_recv, out_sem,
):
    nx, ny, nk, nl = dims
    gx, gy, core = lax.axis_index("gx"), lax.axis_index("gy"), lax.axis_index("comp")
    n_gx, n_gy = lax.axis_size("gx"), lax.axis_size("gy")
    west = (lax.rem(gx + n_gx - 1, n_gx), gy, core)
    east = (lax.rem(gx + 1, n_gx), gy, core)
    south = (gx, lax.rem(gy + n_gy - 1, n_gy), core)
    north = (gx, lax.rem(gy + 1, n_gy), core)
    other = 1 - core
    partner = (gx, gy, other)
    not_first = jnp.where(gy > 0, 1.0, 0.0).astype(F32)
    not_last = jnp.where(gy < n_gy - 1, 1.0, 0.0).astype(F32)

    def rows(start, count):
        return pl.ds(pl.multiple_of(start * ny, ny), count * ny)

    loads = []

    def load(src, dst):
        copy = pltpu.make_async_copy(src, dst, load_sem.at[len(loads)])
        copy.start()
        loads.append(copy)
        return copy

    spec_load = load(spec_hbm, specx.at[pl.ds(ny, nx * ny), :])
    mask_load = load(mask_hbm, maskv)
    cour_load = load(cour_hbm, cour)
    cur_load = load(cur_hbm, curv)
    own_k = pl.ds(pl.multiple_of(core * nk, nk), nk)
    oth_k = pl.ds(pl.multiple_of(other * nk, nk), nk)
    own_l = pl.ds(pl.multiple_of(core * nl, nl), nl)
    late = [
        load(drag_hbm, dragv),
        load(cor_hbm, corv),
        load(proj_hbm.at[0, own_l, own_k], proj.at[pl.ds(0, nl), pl.ds(0, nk)]),
        load(proj_hbm.at[0, own_l, oth_k], proj.at[pl.ds(0, nl), pl.ds(nk, nk)]),
        load(proj_hbm.at[1, own_l, own_k], proj.at[pl.ds(nl, nl), pl.ds(0, nk)]),
        load(proj_hbm.at[1, own_l, oth_k], proj.at[pl.ds(nl, nl), pl.ds(nk, nk)]),
        load(inter_hbm.at[own_k, own_k], wmat.at[pl.ds(0, nk), :]),
        load(inter_hbm.at[oth_k, own_k], wmat.at[pl.ds(nk, nk), :]),
    ]

    barrier = pltpu.get_barrier_semaphore()
    for peer in (west, east, south, north, partner):
        pl.semaphore_signal(barrier, inc=1, device_id=peer, device_id_type=MESH)

    def remote(src, dst, send, recv, peer):
        return pltpu.make_async_remote_copy(
            src_ref=src, dst_ref=dst, send_sem=send, recv_sem=recv,
            device_id=peer, device_id_type=MESH,
        )

    pl.semaphore_wait(barrier, 5)
    hx = [
        remote(spec_hbm.at[rows(0, 1), :], specx.at[rows(nx + 1, 1), :], hx_send.at[0], hx_recv.at[1], west),
        remote(spec_hbm.at[rows(nx - 1, 1), :], specx.at[rows(0, 1), :], hx_send.at[1], hx_recv.at[0], east),
    ]
    for copy in hx:
        copy.start()

    spec_load.wait()
    for x in range(nx):
        first = (1 + x) * ny
        ystage[0, x:x + 1, :] = specx[first:first + 16, :].astype(F32)[0:1]
        ystage[1, x:x + 1, :] = specx[first + ny - 16:first + ny, :].astype(F32)[15:16]
    ysend[...] = ystage[...].astype(BF16)
    hy = [
        remote(ysend.at[0], yrecv.at[1], hy_send.at[0], hy_recv.at[1], south),
        remote(ysend.at[1], yrecv.at[0], hy_send.at[1], hy_recv.at[0], north),
    ]
    for copy in hy:
        copy.start()

    lane = lax.broadcasted_iota(jnp.int32, (nl, ny), 1)
    lev_u, lev_v = pl.ds(0, nl), pl.ds(nl, nl)

    def pack(x, u, v, low, high):
        for c, q in ((0, u), (1, v)):
            spot = c * nx + x
            low = jnp.where(lane == spot, pltpu.roll(q, spot, 1), low)
            high = jnp.where(lane == spot, pltpu.roll(q, spot + 1, 1), high)
        return low, high

    def flow_x(s):
        return [
            remote(flow.at[s, 1], flow.at[s, nx + 1], fx_send.at[s, 0], fx_recv.at[s, 1], west),
            remote(flow.at[s, nx], flow.at[s, 0], fx_send.at[s, 1], fx_recv.at[s, 0], east),
        ]

    def flow_y(s):
        return [
            remote(vsend.at[s, 0], vrecv.at[s, 1], fy_send.at[s, 0], fy_recv.at[s, 1], south),
            remote(vsend.at[s, 1], vrecv.at[s, 0], fy_send.at[s, 1], fy_recv.at[s, 0], north),
        ]

    def send_x(s):
        for copy in flow_x(s):
            copy.start()

    def send_y(s, low, high):
        vsend[s, 0] = low
        vsend[s, 1] = high
        for copy in flow_y(s):
            copy.start()

    zero = jnp.zeros((nl, ny), F32)
    cur_load.wait()

    def first_flow(x, carry):
        u = curv[pl.ds(x, nl, stride=nx), :]
        v = curv[pl.ds(nl * nx + x, nl, stride=nx), :]
        flow[0, x + 1, lev_u, :] = u
        flow[0, x + 1, lev_v, :] = v
        return pack(x, u, v, *carry)

    edges = lax.fori_loop(0, nx, first_flow, (zero, zero), unroll=4)
    send_x(0)
    send_y(0, *edges)

    mask_load.wait()
    cour_load.wait()
    own_mask = maskv[...].astype(F32)
    maskf[...] = own_mask
    turned = jnp.concatenate([own_mask, jnp.zeros((ny - nx, ny), F32)], axis=0).T
    for x in range(nx):
        mask_b[x * ny:(x + 1) * ny, :] = jnp.broadcast_to(turned[:, x:x + 1], (ny, 128))

    for copy in late:
        copy.wait()
    eye = lax.broadcasted_iota(jnp.int32, (nl, nl), 0) == lax.broadcasted_iota(jnp.int32, (nl, nl), 1)
    drag = jnp.sum(jnp.where(eye, jnp.broadcast_to(dragv[...], (nl, nl)), 0.0), axis=1, keepdims=True)
    drag_b[...] = jnp.broadcast_to(drag, (nl, ny))

    chunks = nk // 128
    for copy in hy:
        copy.wait_recv()
    for kc in range(chunks):
        ks = slice(kc * 128, (kc + 1) * 128)
        yhalo[0, kc] = yrecv[0, :, ks].astype(F32) * not_first
        yhalo[1, kc] = yrecv[1, :, ks].astype(F32) * not_last

    def swap(x):
        return remote(
            adv.at[rows(x, 1), pl.ds(0, nk)], adv.at[rows(x, 1), pl.ds(nk, nk)],
            av_send.at[x], av_recv.at[x], partner,
        )

    def advect(x, carry):
        mb = mask_b[rows(x, 1), :]
        for kc in range(chunks):
            ks = slice(kc * 128, (kc + 1) * 128)
            a, b = cour[0:1, ks], cour[1:2, ks]
            mag_a, mag_b = jnp.abs(a), jnp.abs(b)
            here = specx[rows(x + 1, 1), ks].astype(F32)
            fbuf[kc, 8:8 + ny, :] = here
            fbuf[kc, 7:8, :] = yhalo[0, kc, pl.ds(x, 1), :]
            fbuf[kc, 8 + ny:9 + ny, :] = yhalo[1, kc, pl.ds(x, 1), :]
            ux = jnp.where(a > 0, specx[rows(x, 1), ks].astype(F32), specx[rows(x + 2, 1), ks].astype(F32))
            uy = jnp.where(b > 0, fbuf[kc, 7:7 + ny, :], fbuf[kc, 9:9 + ny, :])
            new = (1.0 - mag_a - mag_b) * here + mag_a * ux + mag_b * uy
            adv[rows(x, 1), ks] = (mb * new).astype(BF16)
        swap(x).start()
        return carry

    def drift(p, carry):
        swap(2 * p).wait_recv()
        swap(2 * p + 1).wait_recv()
        both = lax.dot_general(
            proj[...], adv[rows(2 * p, 2), :], (((1,), (1,)), ((), ())),
            preferred_element_type=F32,
        )
        stokes[2 * p] = both[:, :ny]
        stokes[2 * p + 1] = both[:, ny:]
        return carry

    def halo_y(s):
        return vrecv[s, 0] * not_first, vrecv[s, 1] * not_last

    def step(s, south_halo, north_halo, x, carry):
        def sides(c, q):
            spot = c * nx + x
            low = jnp.where(lane == 0, pltpu.roll(south_halo, ny - spot, 1), pltpu.roll(q, 1, 1))
            high = jnp.where(lane == ny - 1, pltpu.roll(north_halo, ny - 1 - spot, 1), pltpu.roll(q, ny - 1, 1))
            return low, high

        u, v = flow[s, x + 1, lev_u, :], flow[s, x + 1, lev_v, :]
        u_w, v_w = flow[s, x, lev_u, :], flow[s, x, lev_v, :]
        u_e, v_e = flow[s, x + 2, lev_u, :], flow[s, x + 2, lev_v, :]
        u_s, u_n = sides(0, u)
        v_s, v_n = sides(1, v)
        drag = drag_b[...]
        total = corv[...] + 0.5 * (v_e - v_w) - 0.5 * (u_n - u_s)
        lap_u = u_e + u_w + u_n + u_s - 4.0 * u
        lap_v = v_e + v_w + v_n + v_s - 4.0 * v
        m = maskf[pl.ds(x, 1), :]
        u_new = m * (u + DT * (total * (v + stokes[x, lev_v, :]) - drag * u + VISC * lap_u))
        v_new = m * (v + DT * (-total * (u + stokes[x, lev_u, :]) - drag * v + VISC * lap_v))
        if s == SUBSTEPS - 1:
            coutv[pl.ds(x, nl, stride=nx), :] = u_new
            coutv[pl.ds(nl * nx + x, nl, stride=nx), :] = v_new
            return carry
        flow[s + 1, x + 1, lev_u, :] = u_new
        flow[s + 1, x + 1, lev_v, :] = v_new
        return pack(x, u_new, v_new, *carry)

    wide = 256

    def put(x):
        return pltpu.make_async_copy(
            obuf.at[rows(x, 2), :], wave_hbm.at[rows(x, 2), :], out_sem.at[x // 2]
        )

    def gain(x, count):
        rs = rows(x, count)
        mb = mask_b[rs, :]
        mb = jnp.concatenate([mb] * (wide // 128), axis=1)
        for n in range(nk // wide):
            ns = slice(n * wide, (n + 1) * wide)
            got = jnp.dot(adv[rs, :], wmat[:, ns], preferred_element_type=F32)
            obuf[rs, ns] = (mb * (adv[rs, ns].astype(F32) + got)).astype(BF16)
        for part in range(0, count, 2):
            put(x + part).start()

    def arrived(copies):
        for copy in copies:
            copy.wait_recv()

    lax.fori_loop(1, nx - 1, advect, 0)
    lax.fori_loop(1, nx // 2 - 1, drift, 0)
    arrived(flow_y(0))
    halo = halo_y(0)
    edges = lax.fori_loop(2, nx - 2, functools.partial(step, 0, *halo), (zero, zero), unroll=2)
    for x in range(4, nx - 4, 4):
        gain(x, 4)

    for copy in hx:
        copy.wait_recv()
    advect(0, 0)
    advect(nx - 1, 0)
    arrived(flow_x(0))
    gain(2, 2)
    drift(0, 0)
    drift(nx // 2 - 1, 0)
    for x in (0, nx - 1):
        edges = step(0, *halo, x, edges)
    send_x(1)
    for x in (1, nx - 2):
        edges = step(0, *halo, x, edges)
    send_y(1, *edges)

    gain(nx - 4, 4)
    arrived(flow_x(1))
    arrived(flow_y(1))
    halo = halo_y(1)
    edges = (zero, zero)
    for x in (0, nx - 1):
        edges = step(1, *halo, x, edges)
    send_x(2)
    edges = lax.fori_loop(1, nx - 1, functools.partial(step, 1, *halo), edges, unroll=2)
    send_y(2, *edges)

    gain(0, 2)
    arrived(flow_x(2))
    arrived(flow_y(2))
    lax.fori_loop(0, nx, functools.partial(step, 2, *halo_y(2)), 0, unroll=2)
    cout = pltpu.make_async_copy(coutv, curo_hbm, out_sem.at[nx // 2])
    cout.start()

    for copy in hy + hx:
        copy.wait_send()
    for s in range(SUBSTEPS):
        for copy in flow_x(s) + flow_y(s):
            copy.wait_send()

    def drain(x, carry):
        swap(x).wait_send()
        return carry

    lax.fori_loop(0, nx, drain, 0)

    def drain_out(g, carry):
        put(2 * g).wait()
        return carry

    lax.fori_loop(0, nx // 2, drain_out, 0)
    cout.wait()


def local(spectrum, sea_mask, courant, interaction, stokes_proj, currents, level_drag):
    nx, ny, nk = spectrum.shape
    nl = currents.shape[1]
    ny_total = lax.axis_size("gy") * ny
    lat_index = lax.axis_index("gy") * ny + jnp.arange(ny)
    coriolis = jnp.sin(jnp.pi * ((lat_index.astype(F32) + 0.5) / ny_total - 0.5))[None, :]
    any_space = pl.BlockSpec(memory_space=pl.ANY)
    dma = pltpu.SemaphoreType.DMA
    wave, cur = pl.pallas_call(
        functools.partial(kernel, (nx, ny, nk, nl)),
        out_shape=(
            jax.ShapeDtypeStruct((nx * ny, nk), BF16),
            jax.ShapeDtypeStruct((2 * nl * nx, ny), F32),
        ),
        in_specs=[any_space] * 8,
        out_specs=(any_space, any_space),
        scratch_shapes=[
            pltpu.VMEM(((nx + 2) * ny, nk), BF16),
            pltpu.VMEM((nx * ny, 2 * nk), BF16),
            pltpu.VMEM((2 * nk, nk), BF16),
            pltpu.VMEM((2 * nl, 2 * nk), BF16),
            pltpu.VMEM((nx, ny), jnp.int32),
            pltpu.VMEM((2, nk), F32),
            pltpu.VMEM((2 * nl * nx, ny), F32),
            pltpu.VMEM((1, nl), F32),
            pltpu.VMEM((1, ny), F32),
            pltpu.VMEM((nx, ny), F32),
            pltpu.VMEM((nx * ny, 128), F32),
            pltpu.VMEM((nl, ny), F32),
            pltpu.VMEM((nk // 128, ny + 16, 128), F32),
            pltpu.VMEM((2, nx, nk), F32),
            pltpu.VMEM((2, nx, nk), BF16),
            pltpu.VMEM((2, nx, nk), BF16),
            pltpu.VMEM((2, nk // 128, nx, 128), F32),
            pltpu.VMEM((SUBSTEPS, nx + 2, 2 * nl, ny), F32),
            pltpu.VMEM((nx, 2 * nl, ny), F32),
            pltpu.VMEM((SUBSTEPS, 2, nl, ny), F32),
            pltpu.VMEM((SUBSTEPS, 2, nl, ny), F32),
            pltpu.VMEM((nx * ny, nk), BF16),
            pltpu.VMEM((2 * nl * nx, ny), F32),
            dma((12,)),
            dma((2,)), dma((2,)), dma((2,)), dma((2,)),
            dma((nx,)), dma((nx,)),
            dma((SUBSTEPS, 2)), dma((SUBSTEPS, 2)), dma((SUBSTEPS, 2)), dma((SUBSTEPS, 2)),
            dma((nx // 2 + 1,)),
        ],
        compiler_params=pltpu.CompilerParams(
            collective_id=0, has_side_effects=True, vmem_limit_bytes=67_000_000
        ),
        name="wave_ocean",
    )(
        spectrum.reshape(nx * ny, nk),
        sea_mask,
        courant,
        interaction,
        jnp.transpose(stokes_proj, (0, 2, 1)),
        currents.reshape(2 * nl * nx, ny),
        level_drag[None, :],
        coriolis,
    )
    return wave.reshape(nx, ny, nk), cur.reshape(2, nl, nx, ny)


def solution(mesh):
    in_specs = (
        P("gx", "gy", "comp"),
        P("gx", "gy"),
        P(None, "comp"),
        P(),
        P(),
        P(None, "comp", "gx", "gy"),
        P("comp"),
    )
    out_specs = (P("gx", "gy", "comp"), P(None, "comp", "gx", "gy"))
    return jax.shard_map(local, mesh=mesh, in_specs=in_specs, out_specs=out_specs, check_vma=False)
```

```python
import functools

import jax
import jax.numpy as jnp
from jax import lax
from jax.experimental import pallas as pl
from jax.experimental.pallas import tpu as pltpu
from jax.sharding import PartitionSpec as P

SUBSTEPS = 3
DT = 0.5
VISC = 0.4
F32 = jnp.float32
BF16 = jnp.bfloat16
MESH = pl.DeviceIdType.MESH


PAD = 8
LANES = 128


def advance(flow, stokes, mask_t, cor_t, drag, ny, i, store):
    block = 32
    for first in range(0, ny, block):
        at = PAD + first
        u, v = (flow[c, i + 1, at:at + block, :] for c in (0, 1))
        u_w, v_w = (flow[c, i, at:at + block, :] for c in (0, 1))
        u_e, v_e = (flow[c, i + 2, at:at + block, :] for c in (0, 1))
        u_s, v_s = (flow[c, i + 1, at - 1:at + block - 1, :] for c in (0, 1))
        u_n, v_n = (flow[c, i + 1, at + 1:at + block + 1, :] for c in (0, 1))
        rs = pl.ds(pl.multiple_of(i * ny + first, block), block)
        total = cor_t[first:first + block, :] + 0.5 * (v_e - v_w) - 0.5 * (u_n - u_s)
        lap_u = u_e + u_w + u_n + u_s - 4.0 * u
        lap_v = v_e + v_w + v_n + v_s - 4.0 * v
        m = mask_t[rs, :]
        u_new = m * (u + DT * (total * (v + stokes[rs, LANES:2 * LANES]) - drag * u + VISC * lap_u))
        v_new = m * (v + DT * (-total * (u + stokes[rs, 0:LANES]) - drag * v + VISC * lap_v))
        store(i, first, block, u_new, v_new)


def kernel(
    dims,
    spec_hbm, mask_hbm, cour_hbm, inter_hbm, proj_hbm, cur_hbm, drag_hbm,
    wave, last, stokes, mask_t, cor_t, drag_t,
    specx, adv, wmat, proj, projp, maskv, cour, curv, dragv,
    mask_b, fbuf, ystage, ysend, yrecv, yhalo,
    flow, xsend, xrecv, vsend, vrecv,
    load_sem, hx_send, hx_recv, hy_send, hy_recv, av_send, av_recv,
    fx_send, fx_recv, fy_send, fy_recv,
):
    nx, ny, nk, nl = dims
    groups = LANES // nl
    tiles = nx // groups
    gx, gy, core = lax.axis_index("gx"), lax.axis_index("gy"), lax.axis_index("comp")
    n_gx, n_gy = lax.axis_size("gx"), lax.axis_size("gy")
    west = (lax.rem(gx + n_gx - 1, n_gx), gy, core)
    east = (lax.rem(gx + 1, n_gx), gy, core)
    south = (gx, lax.rem(gy + n_gy - 1, n_gy), core)
    north = (gx, lax.rem(gy + 1, n_gy), core)
    other = 1 - core
    partner = (gx, gy, other)
    not_first = jnp.where(gy > 0, 1.0, 0.0).astype(F32)
    not_last = jnp.where(gy < n_gy - 1, 1.0, 0.0).astype(F32)
    scope = jax.named_scope

    def rows(start, count):
        return pl.ds(pl.multiple_of(start * ny, ny), count * ny)

    barrier = pltpu.get_barrier_semaphore()
    for peer in (west, east, south, north, partner):
        pl.semaphore_signal(barrier, inc=1, device_id=peer, device_id_type=MESH)

    loads = []

    def load(src, dst):
        copy = pltpu.make_async_copy(src, dst, load_sem.at[len(loads)])
        copy.start()
        loads.append(copy)
        return copy

    spec_load = load(spec_hbm, specx.at[pl.ds(ny, nx * ny), :])
    cur_load = load(cur_hbm, curv)
    mask_load = load(mask_hbm, maskv)
    cour_load = load(cour_hbm, cour)
    own_k = pl.ds(pl.multiple_of(core * nk, nk), nk)
    oth_k = pl.ds(pl.multiple_of(other * nk, nk), nk)
    own_l = pl.ds(pl.multiple_of(core * nl, nl), nl)
    proj_load = [
        load(proj_hbm.at[c, own_l, ks], proj.at[pl.ds(c * nl, nl), pl.ds(half * nk, nk)])
        for c in (0, 1) for half, ks in ((0, own_k), (1, oth_k))
    ]
    drag_load = load(drag_hbm, dragv)
    w_load = [
        load(inter_hbm.at[own_k, own_k], wmat.at[pl.ds(0, nk), :]),
        load(inter_hbm.at[oth_k, own_k], wmat.at[pl.ds(nk, nk), :]),
    ]

    def remote(src, dst, send, recv, peer):
        return pltpu.make_async_remote_copy(
            src_ref=src, dst_ref=dst, send_sem=send, recv_sem=recv,
            device_id=peer, device_id_type=MESH,
        )

    with scope("t_barrier"):
        pl.semaphore_wait(barrier, 5)
    hx = [
        remote(spec_hbm.at[rows(0, 1), :], specx.at[rows(nx + 1, 1), :], hx_send.at[0], hx_recv.at[1], west),
        remote(spec_hbm.at[rows(nx - 1, 1), :], specx.at[rows(0, 1), :], hx_send.at[1], hx_recv.at[0], east),
    ]
    for copy in hx:
        copy.start()

    with scope("t_spec"):
        spec_load.wait()
    for x in range(nx):
        first = (1 + x) * ny
        ystage[0, x:x + 1, :] = specx[first:first + 16, :].astype(F32)[0:1]
        ystage[1, x:x + 1, :] = specx[first + ny - 16:first + ny, :].astype(F32)[15:16]
    ysend[...] = ystage[...].astype(BF16)
    hy = [
        remote(ysend.at[0], yrecv.at[1], hy_send.at[0], hy_recv.at[1], south),
        remote(ysend.at[1], yrecv.at[0], hy_send.at[1], hy_recv.at[0], north),
    ]
    for copy in hy:
        copy.start()

    inner = slice(PAD, PAD + ny)
    lane = lax.broadcasted_iota(jnp.int32, (ny, LANES), 1)
    half_lane = lax.broadcasted_iota(jnp.int32, (ny // 2, LANES), 1)
    half = ny // 2

    def state(s):
        return last if s == SUBSTEPS - 1 else flow.at[s]

    def flow_x(s):
        return [
            remote(xsend.at[s, 0], xrecv.at[s, 1], fx_send.at[s, 0], fx_recv.at[s, 1], west),
            remote(xsend.at[s, 1], xrecv.at[s, 0], fx_send.at[s, 1], fx_recv.at[s, 0], east),
        ]

    def flow_y(s):
        return [
            remote(vsend.at[s, 0], vrecv.at[s, 1], fy_send.at[s, 0], fy_recv.at[s, 1], south),
            remote(vsend.at[s, 1], vrecv.at[s, 0], fy_send.at[s, 1], fy_recv.at[s, 0], north),
        ]

    def turn(q, lanes):
        return pltpu.roll(q, lanes % LANES, 1) if lanes % LANES else q

    def send_flow(s):
        now = state(s)
        for side, tile, group in ((0, 1, 0), (1, tiles, groups - 1)):
            packed = None
            for c in (0, 1):
                for h in (0, 1):
                    g = 2 * c + h
                    part = turn(now[c, tile, PAD + h * half:PAD + (h + 1) * half, :], nl * (g - group))
                    packed = part if packed is None else jnp.where(half_lane >= nl * g, part, packed)
            xsend[s, side] = packed
        for copy in flow_x(s):
            copy.start()
        for c in (0, 1):
            for i in range(tiles):
                r = c * tiles + i
                vsend[s, 0, r:r + 1, :] = now[c, i + 1, PAD:PAD + 1, :]
                vsend[s, 1, r:r + 1, :] = now[c, i + 1, PAD + ny - 1:PAD + ny, :]
        for copy in flow_y(s):
            copy.start()

    def take_flow(s):
        now = state(s)
        for copy in flow_x(s):
            copy.wait_recv()
        for c in (0, 1):
            for h in (0, 1):
                g = 2 * c + h
                rs = slice(PAD + h * half, PAD + (h + 1) * half)
                from_west = turn(xrecv[s, 0], -nl * g)
                from_east = turn(xrecv[s, 1], nl * (groups - 1 - g))
                now[c, 0, rs, :] = jnp.where(half_lane < nl, from_west, turn(now[c, tiles, rs, :], nl))
                now[c, tiles + 1, rs, :] = jnp.where(
                    half_lane >= LANES - nl, from_east, turn(now[c, 1, rs, :], -nl)
                )
        for copy in flow_y(s):
            copy.wait_recv()
        for c in (0, 1):
            for i in range(tiles):
                r = c * tiles + i
                now[c, i + 1, PAD - 1:PAD, :] = vrecv[s, 0, r:r + 1, :] * not_first
                now[c, i + 1, PAD + ny:PAD + ny + 1, :] = vrecv[s, 1, r:r + 1, :] * not_last

    with scope("t_cur"):
        cur_load.wait()
    for c in (0, 1):
        for i in range(tiles):
            tile = jnp.concatenate(
                [curv[pl.ds(c * nl * nx + q * tiles + i, nl, stride=nx), :] for q in range(groups)], axis=0
            )
            flow[0, c, i + 1, inner, :] = tile.T
    send_flow(0)

    mask_load.wait()
    cour_load.wait()
    turned = jnp.concatenate([maskv[...].astype(F32), jnp.zeros((ny - nx, ny), F32)], axis=0).T
    for x in range(nx):
        mask_b[x * ny:(x + 1) * ny, :] = jnp.broadcast_to(turned[:, x:x + 1], (ny, LANES))
    for i in range(tiles):
        mixed = mask_b[i * ny:(i + 1) * ny, :]
        for q in range(1, groups):
            x = q * tiles + i
            mixed = jnp.where(lane >= nl * q, mask_b[x * ny:(x + 1) * ny, :], mixed)
        mask_t[i * ny:(i + 1) * ny, :] = mixed

    lat = (gy * ny + lax.broadcasted_iota(jnp.int32, (ny, LANES), 0)).astype(F32)
    cor_t[...] = jnp.sin(jnp.pi * ((lat + 0.5) / (n_gy * ny) - 0.5))

    with scope("t_late"):
        for copy in proj_load:
            copy.wait()
        drag_load.wait()
        for copy in w_load:
            copy.wait()
    drag = dragv[...]
    drag_t[...] = jnp.broadcast_to(jnp.concatenate([drag] * groups, axis=1), drag_t.shape)
    for q in range(groups):
        projp[q] = jnp.zeros(projp.shape[1:], BF16)
        for c in (0, 1):
            projp[q, c * LANES + q * nl:c * LANES + (q + 1) * nl, :] = proj[c * nl:(c + 1) * nl, :]

    chunks = nk // 128
    with scope("t_hy"):
        for copy in hy:
            copy.wait_recv()
    for kc in range(chunks):
        ks = slice(kc * 128, (kc + 1) * 128)
        yhalo[0, kc] = yrecv[0, :, ks].astype(F32) * not_first
        yhalo[1, kc] = yrecv[1, :, ks].astype(F32) * not_last

    def swap(x):
        return remote(
            adv.at[rows(x, 1), pl.ds(0, nk)], adv.at[rows(x, 1), pl.ds(nk, nk)],
            av_send.at[x], av_recv.at[x], partner,
        )

    def advect(x, carry):
        mb = mask_b[rows(x, 1), :]
        for kc in range(chunks):
            ks = slice(kc * 128, (kc + 1) * 128)
            a, b = cour[0:1, ks], cour[1:2, ks]
            mag_a, mag_b = jnp.abs(a), jnp.abs(b)
            here = specx[rows(x + 1, 1), ks].astype(F32)
            fbuf[kc, 8:8 + ny, :] = here
            fbuf[kc, 7:8, :] = yhalo[0, kc, pl.ds(x, 1), :]
            fbuf[kc, 8 + ny:9 + ny, :] = yhalo[1, kc, pl.ds(x, 1), :]
            ux = jnp.where(a > 0, specx[rows(x, 1), ks].astype(F32), specx[rows(x + 2, 1), ks].astype(F32))
            uy = jnp.where(b > 0, fbuf[kc, 7:7 + ny, :], fbuf[kc, 9:9 + ny, :])
            new = (1.0 - mag_a - mag_b) * here + mag_a * ux + mag_b * uy
            adv[rows(x, 1), ks] = (mb * new).astype(BF16)
        swap(x).start()
        return carry

    def drift(q, fresh):
        for x in range(q * tiles, (q + 1) * tiles):
            swap(x).wait_recv()
        part = lax.dot_general(
            adv[rows(q * tiles, tiles), :], projp[q], (((1,), (1,)), ((), ())),
            preferred_element_type=F32,
        )
        stokes[...] = part if fresh else stokes[...] + part

    drag_row = drag_t[0:1, :]

    def substep(s):
        now, then = state(s), state(s + 1)

        def store(i, first, block, u_new, v_new):
            at = slice(PAD + first, PAD + first + block)
            then[0, i + 1, at, :] = u_new
            then[1, i + 1, at, :] = v_new

        def one(i, carry):
            advance(now, stokes, mask_t, cor_t, drag_row, ny, i, store)
            return carry

        lax.fori_loop(0, tiles, one, 0)

    wide = 256

    def gain(p, carry):
        rs = rows(p * 4, 4)
        mb = mask_b[rs, :]
        mb = jnp.concatenate([mb] * (wide // 128), axis=1)
        for n in range(nk // wide):
            ns = slice(n * wide, (n + 1) * wide)
            got = jnp.dot(adv[rs, :], wmat[:, ns], preferred_element_type=F32)
            wave[rs, ns] = (mb * (adv[rs, ns].astype(F32) + got)).astype(BF16)
        return carry

    with scope("t_advect"):
        lax.fori_loop(1, nx - 1, advect, 0)
    with scope("t_hx"):
        for copy in hx:
            copy.wait_recv()
    with scope("t_edge"):
        for x in (0, nx - 1):
            advect(x, 0)
    with scope("t_drift"):
        for n, q in enumerate(list(range(1, groups - 1)) + [0, groups - 1]):
            drift(q, n == 0)
    with scope("t_take0"):
        take_flow(0)
    with scope("t_sub0"):
        substep(0)
        send_flow(1)
    with scope("t_gainA"):
        lax.fori_loop(0, nx // 4 - 1, gain, 0)
    with scope("t_take1"):
        take_flow(1)
    with scope("t_sub1"):
        substep(1)
        send_flow(2)
    with scope("t_gainB"):
        gain(nx // 4 - 1, 0)
    with scope("t_take2"):
        take_flow(2)

    with scope("t_out"):
        for copy in hy + hx:
            copy.wait_send()
        for s in range(SUBSTEPS):
            for copy in flow_x(s) + flow_y(s):
                copy.wait_send()

        def drain(x, carry):
            swap(x).wait_send()
            return carry

        lax.fori_loop(0, nx, drain, 0)


def finish(
    dims,
    wave, last, stokes, mask_t, cor_t, drag_t,
    wave_hbm, curo_hbm,
    done, coutv, out_sem,
):
    nx, ny, nk, nl = dims
    groups = LANES // nl
    tiles = nx // groups
    put = pltpu.make_async_copy(wave, wave_hbm, out_sem.at[0])
    put.start()
    drag_row = drag_t[0:1, :]

    def store(i, first, block, u_new, v_new):
        done[0, i, first:first + block, :] = u_new
        done[1, i, first:first + block, :] = v_new

    puts = [put]
    for i in range(tiles):
        advance(last, stokes, mask_t, cor_t, drag_row, ny, i, store)
    for c in (0, 1):
        for i in range(tiles):
            tile = done[c, i].T
            for q in range(groups):
                coutv[pl.ds(c * nl * nx + q * tiles + i, nl, stride=nx), :] = tile[q * nl:(q + 1) * nl]
        part = pl.ds(c * nl * nx, nl * nx)
        put = pltpu.make_async_copy(coutv.at[part, :], curo_hbm.at[part, :], out_sem.at[1 + c])
        put.start()
        puts.append(put)
    for put in puts:
        put.wait()


def local(spectrum, sea_mask, courant, interaction, stokes_proj, currents, level_drag):
    nx, ny, nk = spectrum.shape
    nl = currents.shape[1]
    groups = LANES // nl
    tiles = nx // groups
    dims = (nx, ny, nk, nl)
    hbm = pl.BlockSpec(memory_space=pltpu.HBM)
    vmem = pl.BlockSpec(memory_space=pltpu.VMEM)
    dma = pltpu.SemaphoreType.DMA
    between = pl.pallas_call(
        functools.partial(kernel, dims),
        out_shape=(
            jax.ShapeDtypeStruct((nx * ny, nk), BF16),
            jax.ShapeDtypeStruct((2, tiles + 2, ny + 2 * PAD, LANES), F32),
            jax.ShapeDtypeStruct((tiles * ny, 2 * LANES), F32),
            jax.ShapeDtypeStruct((tiles * ny, LANES), F32),
            jax.ShapeDtypeStruct((ny, LANES), F32),
            jax.ShapeDtypeStruct((8, LANES), F32),
        ),
        in_specs=[hbm] * 7,
        out_specs=(vmem,) * 6,
        scratch_shapes=[
            pltpu.VMEM(((nx + 2) * ny, nk), BF16),
            pltpu.VMEM((nx * ny, 2 * nk), BF16),
            pltpu.VMEM((2 * nk, nk), BF16),
            pltpu.VMEM((2 * nl, 2 * nk), BF16),
            pltpu.VMEM((groups, 2 * LANES, 2 * nk), BF16),
            pltpu.VMEM((nx, ny), jnp.int32),
            pltpu.VMEM((2, nk), F32),
            pltpu.VMEM((2 * nl * nx, ny), F32),
            pltpu.VMEM((1, nl), F32),
            pltpu.VMEM((nx * ny, 128), F32),
            pltpu.VMEM((nk // 128, ny + 16, 128), F32),
            pltpu.VMEM((2, nx, nk), F32),
            pltpu.VMEM((2, nx, nk), BF16),
            pltpu.VMEM((2, nx, nk), BF16),
            pltpu.VMEM((2, nk // 128, nx, 128), F32),
            pltpu.VMEM((SUBSTEPS - 1, 2, tiles + 2, ny + 2 * PAD, LANES), F32),
            pltpu.VMEM((SUBSTEPS, 2, ny // 2, LANES), F32),
            pltpu.VMEM((SUBSTEPS, 2, ny // 2, LANES), F32),
            pltpu.VMEM((SUBSTEPS, 2, 2 * tiles, LANES), F32),
            pltpu.VMEM((SUBSTEPS, 2, 2 * tiles, LANES), F32),
            dma((12,)),
            dma((2,)), dma((2,)), dma((2,)), dma((2,)),
            dma((nx,)), dma((nx,)),
            dma((SUBSTEPS, 2)), dma((SUBSTEPS, 2)), dma((SUBSTEPS, 2)), dma((SUBSTEPS, 2)),
        ],
        compiler_params=pltpu.CompilerParams(
            collective_id=0, has_side_effects=True, vmem_limit_bytes=40 * 1024 * 1024
        ),
        name="wave_ocean",
    )(*(pltpu.with_memory_space_constraint(each, pltpu.HBM) for each in (
        spectrum.reshape(nx * ny, nk),
        sea_mask,
        courant,
        interaction,
        jnp.transpose(stokes_proj, (0, 2, 1)),
        currents.reshape(2 * nl * nx, ny),
        level_drag[None, :],
    )))
    wave, cur = pl.pallas_call(
        functools.partial(finish, dims),
        out_shape=(
            jax.ShapeDtypeStruct((nx * ny, nk), BF16),
            jax.ShapeDtypeStruct((2 * nl * nx, ny), F32),
        ),
        in_specs=[vmem] * 6,
        out_specs=(hbm, hbm),
        scratch_shapes=[
            pltpu.VMEM((2, tiles, ny, LANES), F32),
            pltpu.VMEM((2 * nl * nx, ny), F32),
            dma((3,)),
        ],
        compiler_params=pltpu.CompilerParams(vmem_limit_bytes=40 * 1024 * 1024),
        name="last_substep",
    )(*between)
    return wave.reshape(nx, ny, nk), cur.reshape(2, nl, nx, ny)


def solution(mesh):
    in_specs = (
        P("gx", "gy", "comp"),
        P("gx", "gy"),
        P(None, "comp"),
        P(),
        P(),
        P(None, "comp", "gx", "gy"),
        P("comp"),
    )
    out_specs = (P("gx", "gy", "comp"), P(None, "comp", "gx", "gy"))
    return jax.shard_map(local, mesh=mesh, in_specs=in_specs, out_specs=out_specs, check_vma=False)
```

```python
import functools

import jax
import jax.numpy as jnp
from jax import lax
from jax.experimental import pallas as pl
from jax.experimental.pallas import tpu as pltpu
from jax.sharding import PartitionSpec as P

SUBSTEPS = 3
DT = 0.5
VISC = 0.4
F32 = jnp.float32
BF16 = jnp.bfloat16
MESH = pl.DeviceIdType.MESH


PAD = 8
LANES = 128


def advance(flow, stokes, mask_t, cor_t, drag, ny, i, store):
    block = 32
    for first in range(0, ny, block):
        at = PAD + first
        u, v = (flow[c, i + 1, at:at + block, :] for c in (0, 1))
        u_w, v_w = (flow[c, i, at:at + block, :] for c in (0, 1))
        u_e, v_e = (flow[c, i + 2, at:at + block, :] for c in (0, 1))
        u_s, v_s = (flow[c, i + 1, at - 1:at + block - 1, :] for c in (0, 1))
        u_n, v_n = (flow[c, i + 1, at + 1:at + block + 1, :] for c in (0, 1))
        rs = pl.ds(pl.multiple_of(i * ny + first, block), block)
        total = cor_t[first:first + block, :] + 0.5 * (v_e - v_w) - 0.5 * (u_n - u_s)
        lap_u = u_e + u_w + u_n + u_s - 4.0 * u
        lap_v = v_e + v_w + v_n + v_s - 4.0 * v
        m = mask_t[rs, :]
        u_new = m * (u + DT * (total * (v + stokes[rs, LANES:2 * LANES]) - drag * u + VISC * lap_u))
        v_new = m * (v + DT * (-total * (u + stokes[rs, 0:LANES]) - drag * v + VISC * lap_v))
        store(i, first, block, u_new, v_new)


def kernel(
    dims,
    spec_hbm, mask_hbm, cour_hbm, inter_hbm, proj_hbm, cur_hbm, drag_hbm,
    wave, last, stokes, mask_t, cor_t, drag_t,
    specx, adv, wmat, proj, projp, maskv, cour, curv, dragv,
    mask_b, fbuf, fbuf_n, ystage, ysend, yrecv, yhalo,
    flow, xsend, xrecv, vsend, vrecv,
    load_sem, hx_send, hx_recv, hy_send, hy_recv, av_send, av_recv,
    fx_send, fx_recv, fy_send, fy_recv,
):
    nx, ny, nk, nl = dims
    groups = LANES // nl
    tiles = nx // groups
    gx, gy, core = lax.axis_index("gx"), lax.axis_index("gy"), lax.axis_index("comp")
    n_gx, n_gy = lax.axis_size("gx"), lax.axis_size("gy")
    west = (lax.rem(gx + n_gx - 1, n_gx), gy, core)
    east = (lax.rem(gx + 1, n_gx), gy, core)
    south = (gx, lax.rem(gy + n_gy - 1, n_gy), core)
    north = (gx, lax.rem(gy + 1, n_gy), core)
    other = 1 - core
    partner = (gx, gy, other)
    not_first = jnp.where(gy > 0, 1.0, 0.0).astype(F32)
    not_last = jnp.where(gy < n_gy - 1, 1.0, 0.0).astype(F32)
    scope = jax.named_scope

    def rows(start, count):
        return pl.ds(pl.multiple_of(start * ny, ny), count * ny)

    with scope("t_sig"):
        barrier = pltpu.get_barrier_semaphore()
        for peer in (west, east, south, north, partner):
            pl.semaphore_signal(barrier, inc=1, device_id=peer, device_id_type=MESH)

    loads = []

    def load(src, dst):
        copy = pltpu.make_async_copy(src, dst, load_sem.at[len(loads)])
        copy.start()
        loads.append(copy)
        return copy

    def remote(src, dst, send, recv, peer):
        return pltpu.make_async_remote_copy(
            src_ref=src, dst_ref=dst, send_sem=send, recv_sem=recv,
            device_id=peer, device_id_type=MESH,
        )

    with scope("t_load"):
        spec_load = load(spec_hbm, specx.at[pl.ds(ny, nx * ny), :])
    cur_load = load(cur_hbm, curv)
    mask_load = load(mask_hbm, maskv)
    cour_load = load(cour_hbm, cour)
    own_k = pl.ds(pl.multiple_of(core * nk, nk), nk)
    oth_k = pl.ds(pl.multiple_of(other * nk, nk), nk)
    own_l = pl.ds(pl.multiple_of(core * nl, nl), nl)
    proj_load = [
        load(proj_hbm.at[c, own_l, ks], proj.at[pl.ds(c * nl, nl), pl.ds(half * nk, nk)])
        for c in (0, 1) for half, ks in ((0, own_k), (1, oth_k))
    ]
    drag_load = load(drag_hbm, dragv)
    w_load = [
        load(inter_hbm.at[own_k, own_k], wmat.at[pl.ds(0, nk), :]),
        load(inter_hbm.at[oth_k, own_k], wmat.at[pl.ds(nk, nk), :]),
    ]
    with scope("t_spec"):
        spec_load.wait()
    for x in range(nx):
        first = (1 + x) * ny
        ystage[0, x:x + 1, :] = specx[first:first + 16, :].astype(F32)[0:1]
        ystage[1, x:x + 1, :] = specx[first + ny - 16:first + ny, :].astype(F32)[15:16]
    ysend[...] = ystage[...].astype(BF16)
    with scope("t_barrier"):
        pl.semaphore_wait(barrier, 5)
    hy = [
        remote(ysend.at[0], yrecv.at[1], hy_send.at[0], hy_recv.at[1], south),
        remote(ysend.at[1], yrecv.at[0], hy_send.at[1], hy_recv.at[0], north),
    ]
    for copy in hy:
        copy.start()
    hx = [
        remote(spec_hbm.at[rows(0, 1), :], specx.at[rows(nx + 1, 1), :], hx_send.at[0], hx_recv.at[1], west),
        remote(spec_hbm.at[rows(nx - 1, 1), :], specx.at[rows(0, 1), :], hx_send.at[1], hx_recv.at[0], east),
    ]
    for copy in hx:
        copy.start()

    inner = slice(PAD, PAD + ny)
    lane = lax.broadcasted_iota(jnp.int32, (ny, LANES), 1)
    half_lane = lax.broadcasted_iota(jnp.int32, (ny // 2, LANES), 1)
    half = ny // 2

    def state(s):
        return last if s == SUBSTEPS - 1 else flow.at[s]

    def flow_x(s):
        return [
            remote(xsend.at[s, 0], xrecv.at[s, 1], fx_send.at[s, 0], fx_recv.at[s, 1], west),
            remote(xsend.at[s, 1], xrecv.at[s, 0], fx_send.at[s, 1], fx_recv.at[s, 0], east),
        ]

    def flow_y(s):
        return [
            remote(vsend.at[s, 0], vrecv.at[s, 1], fy_send.at[s, 0], fy_recv.at[s, 1], south),
            remote(vsend.at[s, 1], vrecv.at[s, 0], fy_send.at[s, 1], fy_recv.at[s, 0], north),
        ]

    def turn(q, lanes):
        return pltpu.roll(q, lanes % LANES, 1) if lanes % LANES else q

    def send_flow(s):
        now = state(s)
        for c in (0, 1):
            for i in range(tiles):
                r = c * tiles + i
                vsend[s, 0, r:r + 1, :] = now[c, i + 1, PAD:PAD + 1, :]
                vsend[s, 1, r:r + 1, :] = now[c, i + 1, PAD + ny - 1:PAD + ny, :]
        for copy in flow_y(s):
            copy.start()
        for side, tile, group in ((0, 1, 0), (1, tiles, groups - 1)):
            packed = None
            for c in (0, 1):
                for h in (0, 1):
                    g = 2 * c + h
                    part = turn(now[c, tile, PAD + h * half:PAD + (h + 1) * half, :], nl * (g - group))
                    packed = part if packed is None else jnp.where(half_lane >= nl * g, part, packed)
            xsend[s, side] = packed.astype(BF16)
        for copy in flow_x(s):
            copy.start()

    def take_flow(s):
        now = state(s)
        for copy in flow_x(s):
            copy.wait_recv()
        for c in (0, 1):
            for h in (0, 1):
                g = 2 * c + h
                rs = slice(PAD + h * half, PAD + (h + 1) * half)
                from_west = turn(xrecv[s, 0].astype(F32), -nl * g)
                from_east = turn(xrecv[s, 1].astype(F32), nl * (groups - 1 - g))
                now[c, 0, rs, :] = jnp.where(half_lane < nl, from_west, turn(now[c, tiles, rs, :], nl))
                now[c, tiles + 1, rs, :] = jnp.where(
                    half_lane >= LANES - nl, from_east, turn(now[c, 1, rs, :], -nl)
                )
        for copy in flow_y(s):
            copy.wait_recv()
        for c in (0, 1):
            for i in range(tiles):
                r = c * tiles + i
                now[c, i + 1, PAD - 1:PAD, :] = vrecv[s, 0, r:r + 1, :] * not_first
                now[c, i + 1, PAD + ny:PAD + ny + 1, :] = vrecv[s, 1, r:r + 1, :] * not_last

    with scope("t_cur"):
        cur_load.wait()
    for c in (0, 1):
        for i in range(tiles):
            tile = jnp.concatenate(
                [curv[pl.ds(c * nl * nx + q * tiles + i, nl, stride=nx), :] for q in range(groups)], axis=0
            )
            flow[0, c, i + 1, inner, :] = tile.T
    send_flow(0)

    mask_load.wait()
    cour_load.wait()
    turned = jnp.concatenate([maskv[...].astype(F32), jnp.zeros((ny - nx, ny), F32)], axis=0).T
    for x in range(nx):
        mask_b[x * ny:(x + 1) * ny, :] = jnp.broadcast_to(turned[:, x:x + 1], (ny, LANES))
    for i in range(tiles):
        mixed = mask_b[i * ny:(i + 1) * ny, :]
        for q in range(1, groups):
            x = q * tiles + i
            mixed = jnp.where(lane >= nl * q, mask_b[x * ny:(x + 1) * ny, :], mixed)
        mask_t[i * ny:(i + 1) * ny, :] = mixed

    lat = (gy * ny + lax.broadcasted_iota(jnp.int32, (ny, LANES), 0)).astype(F32)
    cor_t[...] = jnp.sin(jnp.pi * ((lat + 0.5) / (n_gy * ny) - 0.5))

    drag_load.wait()
    drag_t[...] = jnp.broadcast_to(jnp.concatenate([dragv[...]] * groups, axis=1), drag_t.shape)

    def finish_loads():
        for copy in w_load:
            copy.wait()

    for copy in proj_load:
        copy.wait()
    proj[2 * nl:LANES, :] = jnp.zeros((LANES - 2 * nl, 2 * nk), BF16)
    for q in range(groups):
        projp[q] = jnp.zeros(projp.shape[1:], BF16)
        for c in (0, 1):
            projp[q, c * LANES + q * nl:c * LANES + (q + 1) * nl, :] = proj[c * nl:(c + 1) * nl, :]

    chunks = nk // 128
    rim = 16

    def swap(x, first, count, part):
        rs = pl.ds(pl.multiple_of(x * ny + first, rim), count)
        return remote(
            adv.at[rs, pl.ds(0, nk)], adv.at[rs, pl.ds(nk, nk)],
            av_send.at[part, x], av_recv.at[part, x], partner,
        )

    def swaps(x, whole):
        if whole:
            return [swap(x, 0, ny, 0)]
        return [swap(x, rim, ny - 2 * rim, 0), swap(x, 0, rim, 1), swap(x, ny - rim, rim, 2)]

    def advect(x, first, count, buf, base):
        rs = pl.ds(pl.multiple_of(x * ny + first, rim), count)
        mb = mask_b[rs, :]
        at = 8 + first - base
        for kc in range(chunks):
            ks = slice(kc * 128, (kc + 1) * 128)
            a, b = cour[0:1, ks], cour[1:2, ks]
            mag_a, mag_b = jnp.abs(a), jnp.abs(b)
            here = buf[kc, at:at + count, :]
            r_w = pl.ds(pl.multiple_of(x * ny + first, rim), count)
            r_e = pl.ds(pl.multiple_of((x + 2) * ny + first, rim), count)
            ux = jnp.where(a > 0, specx[r_w, ks].astype(F32), specx[r_e, ks].astype(F32))
            uy = jnp.where(b > 0, buf[kc, at - 1:at + count - 1, :], buf[kc, at + 1:at + count + 1, :])
            new = (1.0 - mag_a - mag_b) * here + mag_a * ux + mag_b * uy
            adv[rs, ks] = (mb * new).astype(BF16)

    def widen(x, first, count, buf):
        for kc in range(chunks):
            ks = slice(kc * 128, (kc + 1) * 128)
            rs = pl.ds(pl.multiple_of((x + 1) * ny + first, rim), count)
            buf[kc, 8:8 + count, :] = specx[rs, ks].astype(F32)

    def halo_rows(x, side, row, buf):
        for kc in range(chunks):
            buf[kc, row:row + 1, :] = yhalo[side, kc, pl.ds(x, 1), :]

    def advect_middle(x, carry):
        widen(x, 0, ny, fbuf)
        advect(x, rim, ny - 2 * rim, fbuf, 0)
        swap(x, rim, ny - 2 * rim, 0).start()
        return carry

    def advect_rim(x, carry):
        widen(x, 0, 2 * rim, fbuf)
        halo_rows(x, 0, 7, fbuf)
        advect(x, 0, rim, fbuf, 0)
        swap(x, 0, rim, 1).start()
        widen(x, ny - 2 * rim, 2 * rim, fbuf_n)
        halo_rows(x, 1, 8 + 2 * rim, fbuf_n)
        advect(x, ny - rim, rim, fbuf_n, ny - 2 * rim)
        swap(x, ny - rim, rim, 2).start()
        return carry

    def advect_all(x):
        widen(x, 0, ny, fbuf)
        halo_rows(x, 0, 7, fbuf)
        halo_rows(x, 1, 8 + ny, fbuf)
        advect(x, 0, ny, fbuf, 0)
        swap(x, 0, ny, 0).start()

    def drift(x, count, whole, fresh):
        q, tile = x // tiles, x % tiles
        for each in range(x, x + count):
            for copy in swaps(each, whole):
                copy.wait_recv()
        part = lax.dot_general(
            adv[rows(x, count), :], projp[q], (((1,), (1,)), ((), ())),
            preferred_element_type=F32,
        )
        rs = pl.ds(tile * ny, count * ny)
        stokes[rs, :] = part if fresh else stokes[rs, :] + part

    def drift_row(x):
        q, tile = x // tiles, x % tiles
        swap(x, 0, ny, 0).wait_recv()
        part = lax.dot_general(
            adv[rows(x, 1), :], proj[...], (((1,), (1,)), ((), ())), preferred_element_type=F32,
        )
        mine = (lane >= q * nl) & (lane < (q + 1) * nl)
        rs = pl.ds(tile * ny, ny)
        for c in (0, 1):
            ls = slice(c * LANES, (c + 1) * LANES)
            stokes[rs, ls] = stokes[rs, ls] + jnp.where(mine, turn(part, nl * (q - c)), 0.0)

    drag_row = drag_t[0:1, :]

    def substep(s, which):
        now, then = state(s), state(s + 1)

        def store(i, first, block, u_new, v_new):
            at = slice(PAD + first, PAD + first + block)
            then[0, i + 1, at, :] = u_new
            then[1, i + 1, at, :] = v_new

        def one(i, carry):
            advance(now, stokes, mask_t, cor_t, drag_row, ny, i, store)
            return carry

        lax.fori_loop(*which[:2], lambda n, carry: one(which[2] * n, carry), 0)

    wide = 256

    def gain(p, carry):
        rs = rows(p * 4, 4)
        mb = mask_b[rs, :]
        mb = jnp.concatenate([mb] * (wide // 128), axis=1)
        for n in range(nk // wide):
            ns = slice(n * wide, (n + 1) * wide)
            got = jnp.dot(adv[rs, :], wmat[:, ns], preferred_element_type=F32)
            wave[rs, ns] = (mb * (adv[rs, ns].astype(F32) + got)).astype(BF16)
        return carry

    with scope("t_middle"):
        lax.fori_loop(1, nx - 1, advect_middle, 0)
    with scope("t_hy"):
        for copy in hy:
            copy.wait_recv()
    for kc in range(chunks):
        ks = slice(kc * 128, (kc + 1) * 128)
        yhalo[0, kc] = yrecv[0, :, ks].astype(F32) * not_first
        yhalo[1, kc] = yrecv[1, :, ks].astype(F32) * not_last
    with scope("t_rim"):
        lax.fori_loop(1, nx - 1, advect_rim, 0)
    with scope("t_late"):
        finish_loads()
    with scope("t_drift"):
        for q in range(1, groups - 1):
            drift(q * tiles, tiles, False, q == 1)
    with scope("t_hx"):
        for copy in hx:
            copy.wait_recv()
    with scope("t_edge"):
        advect_all(0)
        advect_all(nx - 1)
    with scope("t_drift3"):
        drift(1, tiles - 1, False, False)
        drift(nx - tiles, tiles - 1, False, False)
    with scope("t_take0"):
        take_flow(0)
    with scope("t_sub0a"):
        substep(0, (1, tiles - 1, 1))
    with scope("t_driftE"):
        drift_row(0)
        drift_row(nx - 1)
    with scope("t_sub0b"):
        substep(0, (0, 2, tiles - 1))
        send_flow(1)
    with scope("t_gainA"):
        lax.fori_loop(1, nx // 4, gain, 0)
    with scope("t_take1"):
        take_flow(1)
    with scope("t_sub1"):
        substep(1, (0, tiles, 1))
        send_flow(2)
    with scope("t_gainB"):
        gain(0, 0)
    with scope("t_take2"):
        take_flow(2)

    with scope("t_out"):
        for copy in hy + hx:
            copy.wait_send()
        for s in range(SUBSTEPS):
            for copy in flow_x(s) + flow_y(s):
                copy.wait_send()

        def drain(x, carry):
            for copy in swaps(x, False):
                copy.wait_send()
            return carry

        lax.fori_loop(1, nx - 1, drain, 0)
        for x in (0, nx - 1):
            swap(x, 0, ny, 0).wait_send()


def finish(
    dims,
    wave, last, stokes, mask_t, cor_t, drag_t,
    wave_hbm, curo_hbm,
    done, coutv, out_sem,
):
    nx, ny, nk, nl = dims
    groups = LANES // nl
    tiles = nx // groups
    put = pltpu.make_async_copy(wave, wave_hbm, out_sem.at[0])
    put.start()
    drag_row = drag_t[0:1, :]

    def store(i, first, block, u_new, v_new):
        done[0, i, first:first + block, :] = u_new
        done[1, i, first:first + block, :] = v_new

    puts = [put]
    for i in range(tiles):
        advance(last, stokes, mask_t, cor_t, drag_row, ny, i, store)
    for c in (0, 1):
        for i in range(tiles):
            tile = done[c, i].T
            for q in range(groups):
                coutv[pl.ds(c * nl * nx + q * tiles + i, nl, stride=nx), :] = tile[q * nl:(q + 1) * nl]
        part = pl.ds(c * nl * nx, nl * nx)
        put = pltpu.make_async_copy(coutv.at[part, :], curo_hbm.at[part, :], out_sem.at[1 + c])
        put.start()
        puts.append(put)
    for put in puts:
        put.wait()


def local(spectrum, sea_mask, courant, interaction, stokes_proj, currents, level_drag):
    nx, ny, nk = spectrum.shape
    nl = currents.shape[1]
    groups = LANES // nl
    tiles = nx // groups
    dims = (nx, ny, nk, nl)
    hbm = pl.BlockSpec(memory_space=pltpu.HBM)
    vmem = pl.BlockSpec(memory_space=pltpu.VMEM)
    dma = pltpu.SemaphoreType.DMA
    between = pl.pallas_call(
        functools.partial(kernel, dims),
        out_shape=(
            jax.ShapeDtypeStruct((nx * ny, nk), BF16),
            jax.ShapeDtypeStruct((2, tiles + 2, ny + 2 * PAD, LANES), F32),
            jax.ShapeDtypeStruct((tiles * ny, 2 * LANES), F32),
            jax.ShapeDtypeStruct((tiles * ny, LANES), F32),
            jax.ShapeDtypeStruct((ny, LANES), F32),
            jax.ShapeDtypeStruct((8, LANES), F32),
        ),
        in_specs=[hbm] * 7,
        out_specs=(vmem,) * 6,
        scratch_shapes=[
            pltpu.VMEM(((nx + 2) * ny, nk), BF16),
            pltpu.VMEM((nx * ny, 2 * nk), BF16),
            pltpu.VMEM((2 * nk, nk), BF16),
            pltpu.VMEM((LANES, 2 * nk), BF16),
            pltpu.VMEM((groups, 2 * LANES, 2 * nk), BF16),
            pltpu.VMEM((nx, ny), jnp.int32),
            pltpu.VMEM((2, nk), F32),
            pltpu.VMEM((2 * nl * nx, ny), F32),
            pltpu.VMEM((1, nl), F32),
            pltpu.VMEM((nx * ny, 128), F32),
            pltpu.VMEM((nk // 128, ny + 16, 128), F32),
            pltpu.VMEM((nk // 128, 48, 128), F32),
            pltpu.VMEM((2, nx, nk), F32),
            pltpu.VMEM((2, nx, nk), BF16),
            pltpu.VMEM((2, nx, nk), BF16),
            pltpu.VMEM((2, nk // 128, nx, 128), F32),
            pltpu.VMEM((SUBSTEPS - 1, 2, tiles + 2, ny + 2 * PAD, LANES), F32),
            pltpu.VMEM((SUBSTEPS, 2, ny // 2, LANES), BF16),
            pltpu.VMEM((SUBSTEPS, 2, ny // 2, LANES), BF16),
            pltpu.VMEM((SUBSTEPS, 2, 2 * tiles, LANES), F32),
            pltpu.VMEM((SUBSTEPS, 2, 2 * tiles, LANES), F32),
            dma((12,)),
            dma((2,)), dma((2,)), dma((2,)), dma((2,)),
            dma((3, nx)), dma((3, nx)),
            dma((SUBSTEPS, 2)), dma((SUBSTEPS, 2)), dma((SUBSTEPS, 2)), dma((SUBSTEPS, 2)),
        ],
        compiler_params=pltpu.CompilerParams(
            collective_id=0, has_side_effects=True, vmem_limit_bytes=40 * 1024 * 1024
        ),
        name="wave_ocean",
    )(*(pltpu.with_memory_space_constraint(each, pltpu.HBM) for each in (
        spectrum.reshape(nx * ny, nk),
        sea_mask,
        courant,
        interaction,
        jnp.transpose(stokes_proj, (0, 2, 1)),
        currents.reshape(2 * nl * nx, ny),
        level_drag[None, :],
    )))
    wave, cur = pl.pallas_call(
        functools.partial(finish, dims),
        out_shape=(
            jax.ShapeDtypeStruct((nx * ny, nk), BF16),
            jax.ShapeDtypeStruct((2 * nl * nx, ny), F32),
        ),
        in_specs=[vmem] * 6,
        out_specs=(hbm, hbm),
        scratch_shapes=[
            pltpu.VMEM((2, tiles, ny, LANES), F32),
            pltpu.VMEM((2 * nl * nx, ny), F32),
            dma((3,)),
        ],
        compiler_params=pltpu.CompilerParams(vmem_limit_bytes=40 * 1024 * 1024),
        name="last_substep",
    )(*between)
    return wave.reshape(nx, ny, nk), cur.reshape(2, nl, nx, ny)


def solution(mesh):
    in_specs = (
        P("gx", "gy", "comp"),
        P("gx", "gy"),
        P(None, "comp"),
        P(),
        P(),
        P(None, "comp", "gx", "gy"),
        P("comp"),
    )
    out_specs = (P("gx", "gy", "comp"), P(None, "comp", "gx", "gy"))
    return jax.shard_map(local, mesh=mesh, in_specs=in_specs, out_specs=out_specs, check_vma=False)
```

```python
import functools

import jax
import jax.numpy as jnp
from jax import lax
from jax.experimental import pallas as pl
from jax.experimental.pallas import tpu as pltpu
from jax.sharding import PartitionSpec as P

SUBSTEPS = 3
DT = 0.5
VISC = 0.4
F32 = jnp.float32
BF16 = jnp.bfloat16
MESH = pl.DeviceIdType.MESH


PAD = 8
LANES = 128


def advance(flow, stokes, mask_t, cor_t, drag, ny, i, store):
    block = 32
    for first in range(0, ny, block):
        at = PAD + first
        u, v = (flow[c, i + 1, at:at + block, :] for c in (0, 1))
        u_w, v_w = (flow[c, i, at:at + block, :] for c in (0, 1))
        u_e, v_e = (flow[c, i + 2, at:at + block, :] for c in (0, 1))
        u_s, v_s = (flow[c, i + 1, at - 1:at + block - 1, :] for c in (0, 1))
        u_n, v_n = (flow[c, i + 1, at + 1:at + block + 1, :] for c in (0, 1))
        rs = pl.ds(pl.multiple_of(i * ny + first, block), block)
        total = cor_t[first:first + block, :] + 0.5 * (v_e - v_w) - 0.5 * (u_n - u_s)
        lap_u = u_e + u_w + u_n + u_s - 4.0 * u
        lap_v = v_e + v_w + v_n + v_s - 4.0 * v
        m = mask_t[rs, :]
        u_new = m * (u + DT * (total * (v + stokes[rs, LANES:2 * LANES]) - drag * u + VISC * lap_u))
        v_new = m * (v + DT * (-total * (u + stokes[rs, 0:LANES]) - drag * v + VISC * lap_v))
        store(i, first, block, u_new, v_new)


def kernel(
    dims,
    spec_hbm, mask_hbm, cour_hbm, inter_hbm, proj_hbm, cur_hbm, drag_hbm,
    wave, last, stokes, mask_t, cor_t, drag_t,
    specx, adv, wmat, proj, projp, maskv, cour, curv, dragv,
    mask_b, fbuf, fbuf_n, ystage, ysend, yrecv, yhalo,
    flow, xsend, xrecv, vsend, vrecv,
    load_sem, hx_send, hx_recv, hy_send, hy_recv, av_send, av_recv,
    fx_send, fx_recv, fy_send, fy_recv,
):
    nx, ny, nk, nl = dims
    groups = LANES // nl
    tiles = nx // groups
    gx, gy, core = lax.axis_index("gx"), lax.axis_index("gy"), lax.axis_index("comp")
    n_gx, n_gy = lax.axis_size("gx"), lax.axis_size("gy")
    west = (lax.rem(gx + n_gx - 1, n_gx), gy, core)
    east = (lax.rem(gx + 1, n_gx), gy, core)
    south = (gx, lax.rem(gy + n_gy - 1, n_gy), core)
    north = (gx, lax.rem(gy + 1, n_gy), core)
    other = 1 - core
    partner = (gx, gy, other)
    not_first = jnp.where(gy > 0, 1.0, 0.0).astype(F32)
    not_last = jnp.where(gy < n_gy - 1, 1.0, 0.0).astype(F32)
    scope = jax.named_scope

    def rows(start, count):
        return pl.ds(pl.multiple_of(start * ny, ny), count * ny)

    with scope("t_sig"):
        barrier = pltpu.get_barrier_semaphore()
        for peer in (west, east, south, north, partner):
            pl.semaphore_signal(barrier, inc=1, device_id=peer, device_id_type=MESH)

    loads = []

    def load(src, dst):
        copy = pltpu.make_async_copy(src, dst, load_sem.at[len(loads)])
        copy.start()
        loads.append(copy)
        return copy

    def remote(src, dst, send, recv, peer):
        return pltpu.make_async_remote_copy(
            src_ref=src, dst_ref=dst, send_sem=send, recv_sem=recv,
            device_id=peer, device_id_type=MESH,
        )

    rim = 16
    rim_load = [
        load(spec_hbm.at[:, pl.ds(first, rim), :], specx.at[pl.ds(1, nx), pl.ds(first, rim), :])
        for first in (0, ny - rim)
    ]
    cur_load = load(cur_hbm, curv)
    mask_load = load(mask_hbm, maskv)
    cour_load = load(cour_hbm, cour)
    middle = pl.ds(rim, ny - 2 * rim)
    spec_load = load(spec_hbm.at[:, middle, :], specx.at[pl.ds(1, nx), middle, :])
    own_k = pl.ds(pl.multiple_of(core * nk, nk), nk)
    oth_k = pl.ds(pl.multiple_of(other * nk, nk), nk)
    own_l = pl.ds(pl.multiple_of(core * nl, nl), nl)
    proj_load = [
        load(proj_hbm.at[c, own_l, ks], proj.at[pl.ds(c * nl, nl), pl.ds(half * nk, nk)])
        for c in (0, 1) for half, ks in ((0, own_k), (1, oth_k))
    ]
    drag_load = load(drag_hbm, dragv)
    w_load = [
        load(inter_hbm.at[own_k, own_k], wmat.at[pl.ds(0, nk), :]),
        load(inter_hbm.at[oth_k, own_k], wmat.at[pl.ds(nk, nk), :]),
    ]
    with scope("t_spec"):
        for copy in rim_load:
            copy.wait()
    for x in range(nx):
        ystage[0, x:x + 1, :] = specx[1 + x, 0:rim, :].astype(F32)[0:1]
        ystage[1, x:x + 1, :] = specx[1 + x, ny - rim:ny, :].astype(F32)[rim - 1:rim]
    ysend[...] = ystage[...].astype(BF16)
    with scope("t_barrier"):
        pl.semaphore_wait(barrier, 5)
    hy = [
        remote(ysend.at[0], yrecv.at[1], hy_send.at[0], hy_recv.at[1], south),
        remote(ysend.at[1], yrecv.at[0], hy_send.at[1], hy_recv.at[0], north),
    ]
    for copy in hy:
        copy.start()
    def edge_of(n):
        return lax.rem(lax.rem(gx, 2) + n, 2)

    def hx(n):
        f = edge_of(n)
        peer = (lax.rem(gx + n_gx - 1 + 2 * f, n_gx), gy, core)
        return remote(
            spec_hbm.at[f * (nx - 1)], specx.at[(1 - f) * (nx + 1)],
            hx_send.at[n], hx_recv.at[n], peer,
        )

    for n in (0, 1):
        hx(n).start()

    inner = slice(PAD, PAD + ny)
    lane = lax.broadcasted_iota(jnp.int32, (ny, LANES), 1)
    half_lane = lax.broadcasted_iota(jnp.int32, (ny // 2, LANES), 1)
    half = ny // 2

    def state(s):
        return last if s == SUBSTEPS - 1 else flow.at[s]

    def flow_x(s):
        return [
            remote(xsend.at[s, 0], xrecv.at[s, 1], fx_send.at[s, 0], fx_recv.at[s, 1], west),
            remote(xsend.at[s, 1], xrecv.at[s, 0], fx_send.at[s, 1], fx_recv.at[s, 0], east),
        ]

    def flow_y(s):
        return [
            remote(vsend.at[s, 0], vrecv.at[s, 1], fy_send.at[s, 0], fy_recv.at[s, 1], south),
            remote(vsend.at[s, 1], vrecv.at[s, 0], fy_send.at[s, 1], fy_recv.at[s, 0], north),
        ]

    def turn(q, lanes):
        return pltpu.roll(q, lanes % LANES, 1) if lanes % LANES else q

    def send_flow(s):
        now = state(s)
        for c in (0, 1):
            for i in range(tiles):
                r = c * tiles + i
                vsend[s, 0, r:r + 1, :] = now[c, i + 1, PAD:PAD + 1, :]
                vsend[s, 1, r:r + 1, :] = now[c, i + 1, PAD + ny - 1:PAD + ny, :]
        for copy in flow_y(s):
            copy.start()
        for side, tile, group in ((0, 1, 0), (1, tiles, groups - 1)):
            packed = None
            for c in (0, 1):
                for h in (0, 1):
                    g = 2 * c + h
                    part = turn(now[c, tile, PAD + h * half:PAD + (h + 1) * half, :], nl * (g - group))
                    packed = part if packed is None else jnp.where(half_lane >= nl * g, part, packed)
            xsend[s, side] = packed.astype(BF16)
        for copy in flow_x(s):
            copy.start()

    def take_flow(s):
        now = state(s)
        for copy in flow_x(s):
            copy.wait_recv()
        for c in (0, 1):
            for h in (0, 1):
                g = 2 * c + h
                rs = slice(PAD + h * half, PAD + (h + 1) * half)
                from_west = turn(xrecv[s, 0].astype(F32), -nl * g)
                from_east = turn(xrecv[s, 1].astype(F32), nl * (groups - 1 - g))
                now[c, 0, rs, :] = jnp.where(half_lane < nl, from_west, turn(now[c, tiles, rs, :], nl))
                now[c, tiles + 1, rs, :] = jnp.where(
                    half_lane >= LANES - nl, from_east, turn(now[c, 1, rs, :], -nl)
                )
        for copy in flow_y(s):
            copy.wait_recv()
        for c in (0, 1):
            for i in range(tiles):
                r = c * tiles + i
                now[c, i + 1, PAD - 1:PAD, :] = vrecv[s, 0, r:r + 1, :] * not_first
                now[c, i + 1, PAD + ny:PAD + ny + 1, :] = vrecv[s, 1, r:r + 1, :] * not_last

    with scope("t_cur"):
        cur_load.wait()
    for c in (0, 1):
        for i in range(tiles):
            tile = jnp.concatenate(
                [curv[pl.ds(c * nl * nx + q * tiles + i, nl, stride=nx), :] for q in range(groups)], axis=0
            )
            flow[0, c, i + 1, inner, :] = tile.T
    send_flow(0)

    mask_load.wait()
    cour_load.wait()
    turned = jnp.concatenate([maskv[...].astype(F32), jnp.zeros((ny - nx, ny), F32)], axis=0).T
    for x in range(nx):
        mask_b[x * ny:(x + 1) * ny, :] = jnp.broadcast_to(turned[:, x:x + 1], (ny, LANES))
    for i in range(tiles):
        mixed = mask_b[i * ny:(i + 1) * ny, :]
        for q in range(1, groups):
            x = q * tiles + i
            mixed = jnp.where(lane >= nl * q, mask_b[x * ny:(x + 1) * ny, :], mixed)
        mask_t[i * ny:(i + 1) * ny, :] = mixed

    lat = (gy * ny + lax.broadcasted_iota(jnp.int32, (ny, LANES), 0)).astype(F32)
    cor_t[...] = jnp.sin(jnp.pi * ((lat + 0.5) / (n_gy * ny) - 0.5))

    drag_load.wait()
    drag_t[...] = jnp.broadcast_to(jnp.concatenate([dragv[...]] * groups, axis=1), drag_t.shape)

    def finish_loads():
        for copy in w_load:
            copy.wait()

    for copy in proj_load:
        copy.wait()
    proj[2 * nl:LANES, :] = jnp.zeros((LANES - 2 * nl, 2 * nk), BF16)
    for q in range(groups):
        projp[q] = jnp.zeros(projp.shape[1:], BF16)
        for c in (0, 1):
            projp[q, c * LANES + q * nl:c * LANES + (q + 1) * nl, :] = proj[c * nl:(c + 1) * nl, :]

    chunks = nk // 128

    def swap(x, first, count, part):
        rs = pl.ds(pl.multiple_of(x * ny + first, rim), count)
        return remote(
            adv.at[rs, pl.ds(0, nk)], adv.at[rs, pl.ds(nk, nk)],
            av_send.at[part, x], av_recv.at[part, x], partner,
        )

    def swaps(x):
        return [swap(x, rim, ny - 2 * rim, 0), swap(x, 0, rim, 1), swap(x, ny - rim, rim, 2)]

    def advect(x, first, count, buf, base):
        rs = pl.ds(pl.multiple_of(x * ny + first, rim), count)
        mb = mask_b[rs, :]
        at = 8 + first - base
        for kc in range(chunks):
            ks = slice(kc * 128, (kc + 1) * 128)
            a, b = cour[0:1, ks], cour[1:2, ks]
            mag_a, mag_b = jnp.abs(a), jnp.abs(b)
            here = buf[kc, at:at + count, :]
            ys = slice(first, first + count)
            ux = jnp.where(a > 0, specx[x, ys, ks].astype(F32), specx[x + 2, ys, ks].astype(F32))
            uy = jnp.where(b > 0, buf[kc, at - 1:at + count - 1, :], buf[kc, at + 1:at + count + 1, :])
            new = (1.0 - mag_a - mag_b) * here + mag_a * ux + mag_b * uy
            adv[rs, ks] = (mb * new).astype(BF16)

    def widen(x, first, count, buf):
        for kc in range(chunks):
            ks = slice(kc * 128, (kc + 1) * 128)
            buf[kc, 8:8 + count, :] = specx[x + 1, first:first + count, ks].astype(F32)

    def halo_rows(x, side, row, buf):
        for kc in range(chunks):
            buf[kc, row:row + 1, :] = yhalo[side, kc, pl.ds(x, 1), :]

    def advect_middle(x, carry):
        widen(x, 0, ny, fbuf)
        advect(x, rim, ny - 2 * rim, fbuf, 0)
        swap(x, rim, ny - 2 * rim, 0).start()
        return carry

    def advect_rim(x, carry):
        widen(x, 0, 2 * rim, fbuf)
        halo_rows(x, 0, 7, fbuf)
        advect(x, 0, rim, fbuf, 0)
        swap(x, 0, rim, 1).start()
        widen(x, ny - 2 * rim, 2 * rim, fbuf_n)
        halo_rows(x, 1, 8 + 2 * rim, fbuf_n)
        advect(x, ny - rim, rim, fbuf_n, ny - 2 * rim)
        swap(x, ny - rim, rim, 2).start()
        return carry

    def advect_edge(n, carry):
        hx(n).wait_recv()
        x = edge_of(n) * (nx - 1)
        widen(x, 0, ny, fbuf)
        halo_rows(x, 0, 7, fbuf)
        halo_rows(x, 1, 8 + ny, fbuf)
        advect(x, 0, ny, fbuf, 0)
        swap(x, 0, ny, 0).start()
        return carry

    def drift(x, count, fresh):
        q, tile = x // tiles, x % tiles
        for each in range(x, x + count):
            for copy in swaps(each):
                copy.wait_recv()
        part = lax.dot_general(
            adv[rows(x, count), :], projp[q], (((1,), (1,)), ((), ())),
            preferred_element_type=F32,
        )
        rs = pl.ds(tile * ny, count * ny)
        stokes[rs, :] = part if fresh else stokes[rs, :] + part

    def drift_row(n, carry):
        f = edge_of(n)
        x, q, tile = f * (nx - 1), f * (groups - 1), f * (tiles - 1)
        swap(x, 0, ny, 0).wait_recv()
        part = lax.dot_general(
            adv[rows(x, 1), :], proj[...], (((1,), (1,)), ((), ())), preferred_element_type=F32,
        )
        mine = (lane >= q * nl) & (lane < (q + 1) * nl)
        rs = rows(tile, 1)
        for c in (0, 1):
            ls = slice(c * LANES, (c + 1) * LANES)
            moved = pltpu.roll(part, lax.rem(nl * q + LANES - nl * c, LANES), 1)
            stokes[rs, ls] = stokes[rs, ls] + jnp.where(mine, moved, 0.0)
        return carry

    drag_row = drag_t[0:1, :]

    def substep(s):
        now, then = state(s), state(s + 1)

        def store(i, first, block, u_new, v_new):
            at = slice(PAD + first, PAD + first + block)
            then[0, i + 1, at, :] = u_new
            then[1, i + 1, at, :] = v_new

        def one(i, carry):
            advance(now, stokes, mask_t, cor_t, drag_row, ny, i, store)
            return carry

        lax.fori_loop(0, tiles, one, 0)

    wide = 256

    def gain(p, carry):
        rs = rows(p * 4, 4)
        mb = mask_b[rs, :]
        mb = jnp.concatenate([mb] * (wide // 128), axis=1)
        for n in range(nk // wide):
            ns = slice(n * wide, (n + 1) * wide)
            got = jnp.dot(adv[rs, :], wmat[:, ns], preferred_element_type=F32)
            wave[rs, ns] = (mb * (adv[rs, ns].astype(F32) + got)).astype(BF16)
        return carry

    spec_load.wait()
    with scope("t_middle"):
        lax.fori_loop(1, nx - 1, advect_middle, 0)
    with scope("t_hy"):
        for copy in hy:
            copy.wait_recv()
    for kc in range(chunks):
        ks = slice(kc * 128, (kc + 1) * 128)
        yhalo[0, kc] = yrecv[0, :, ks].astype(F32) * not_first
        yhalo[1, kc] = yrecv[1, :, ks].astype(F32) * not_last
    with scope("t_rim"):
        lax.fori_loop(1, nx - 1, advect_rim, 0)
    with scope("t_late"):
        finish_loads()
    with scope("t_drift"):
        for q in range(1, groups - 1):
            drift(q * tiles, tiles, q == 1)
        drift(1, tiles - 1, False)
        drift(nx - tiles, tiles - 1, False)
    with scope("t_hx"):
        lax.fori_loop(0, 2, advect_edge, 0)
    with scope("t_driftE"):
        lax.fori_loop(0, 2, drift_row, 0)
    with scope("t_take0"):
        take_flow(0)
    with scope("t_sub0"):
        substep(0)
        send_flow(1)
    with scope("t_gainA"):
        lax.fori_loop(1, nx // 4, gain, 0)
    with scope("t_take1"):
        take_flow(1)
    with scope("t_sub1"):
        substep(1)
        send_flow(2)
    with scope("t_gainB"):
        gain(0, 0)
    with scope("t_take2"):
        take_flow(2)

    with scope("t_out"):
        for copy in hy + [hx(0), hx(1)]:
            copy.wait_send()
        for s in range(SUBSTEPS):
            for copy in flow_x(s) + flow_y(s):
                copy.wait_send()

        def drain(x, carry):
            for copy in swaps(x):
                copy.wait_send()
            return carry

        lax.fori_loop(1, nx - 1, drain, 0)
        for x in (0, nx - 1):
            swap(x, 0, ny, 0).wait_send()


def finish(
    dims,
    wave, last, stokes, mask_t, cor_t, drag_t,
    wave_hbm, curo_hbm,
    done, coutv, out_sem,
):
    nx, ny, nk, nl = dims
    groups = LANES // nl
    tiles = nx // groups
    put = pltpu.make_async_copy(wave, wave_hbm, out_sem.at[0])
    put.start()
    drag_row = drag_t[0:1, :]

    def store(i, first, block, u_new, v_new):
        done[0, i, first:first + block, :] = u_new
        done[1, i, first:first + block, :] = v_new

    puts = [put]
    for i in range(tiles):
        advance(last, stokes, mask_t, cor_t, drag_row, ny, i, store)
    for c in (0, 1):
        for i in range(tiles):
            tile = done[c, i].T
            for q in range(groups):
                coutv[pl.ds(c * nl * nx + q * tiles + i, nl, stride=nx), :] = tile[q * nl:(q + 1) * nl]
        part = pl.ds(c * nl * nx, nl * nx)
        put = pltpu.make_async_copy(coutv.at[part, :], curo_hbm.at[part, :], out_sem.at[1 + c])
        put.start()
        puts.append(put)
    for put in puts:
        put.wait()


def local(spectrum, sea_mask, courant, interaction, stokes_proj, currents, level_drag):
    nx, ny, nk = spectrum.shape
    nl = currents.shape[1]
    groups = LANES // nl
    tiles = nx // groups
    dims = (nx, ny, nk, nl)
    hbm = pl.BlockSpec(memory_space=pltpu.HBM)
    vmem = pl.BlockSpec(memory_space=pltpu.VMEM)
    dma = pltpu.SemaphoreType.DMA
    between = pl.pallas_call(
        functools.partial(kernel, dims),
        out_shape=(
            jax.ShapeDtypeStruct((nx * ny, nk), BF16),
            jax.ShapeDtypeStruct((2, tiles + 2, ny + 2 * PAD, LANES), F32),
            jax.ShapeDtypeStruct((tiles * ny, 2 * LANES), F32),
            jax.ShapeDtypeStruct((tiles * ny, LANES), F32),
            jax.ShapeDtypeStruct((ny, LANES), F32),
            jax.ShapeDtypeStruct((8, LANES), F32),
        ),
        in_specs=[hbm] * 7,
        out_specs=(vmem,) * 6,
        scratch_shapes=[
            pltpu.VMEM((nx + 2, ny, nk), BF16),
            pltpu.VMEM((nx * ny, 2 * nk), BF16),
            pltpu.VMEM((2 * nk, nk), BF16),
            pltpu.VMEM((LANES, 2 * nk), BF16),
            pltpu.VMEM((groups, 2 * LANES, 2 * nk), BF16),
            pltpu.VMEM((nx, ny), jnp.int32),
            pltpu.VMEM((2, nk), F32),
            pltpu.VMEM((2 * nl * nx, ny), F32),
            pltpu.VMEM((1, nl), F32),
            pltpu.VMEM((nx * ny, 128), F32),
            pltpu.VMEM((nk // 128, ny + 16, 128), F32),
            pltpu.VMEM((nk // 128, 48, 128), F32),
            pltpu.VMEM((2, nx, nk), F32),
            pltpu.VMEM((2, nx, nk), BF16),
            pltpu.VMEM((2, nx, nk), BF16),
            pltpu.VMEM((2, nk // 128, nx, 128), F32),
            pltpu.VMEM((SUBSTEPS - 1, 2, tiles + 2, ny + 2 * PAD, LANES), F32),
            pltpu.VMEM((SUBSTEPS, 2, ny // 2, LANES), BF16),
            pltpu.VMEM((SUBSTEPS, 2, ny // 2, LANES), BF16),
            pltpu.VMEM((SUBSTEPS, 2, 2 * tiles, LANES), F32),
            pltpu.VMEM((SUBSTEPS, 2, 2 * tiles, LANES), F32),
            dma((14,)),
            dma((2,)), dma((2,)), dma((2,)), dma((2,)),
            dma((3, nx)), dma((3, nx)),
            dma((SUBSTEPS, 2)), dma((SUBSTEPS, 2)), dma((SUBSTEPS, 2)), dma((SUBSTEPS, 2)),
        ],
        compiler_params=pltpu.CompilerParams(
            collective_id=0, has_side_effects=True, vmem_limit_bytes=40 * 1024 * 1024
        ),
        name="wave_ocean",
    )(*(pltpu.with_memory_space_constraint(each, pltpu.HBM) for each in (
        spectrum,
        sea_mask,
        courant,
        interaction,
        jnp.transpose(stokes_proj, (0, 2, 1)),
        currents.reshape(2 * nl * nx, ny),
        level_drag[None, :],
    )))
    wave, cur = pl.pallas_call(
        functools.partial(finish, dims),
        out_shape=(
            jax.ShapeDtypeStruct((nx * ny, nk), BF16),
            jax.ShapeDtypeStruct((2 * nl * nx, ny), F32),
        ),
        in_specs=[vmem] * 6,
        out_specs=(hbm, hbm),
        scratch_shapes=[
            pltpu.VMEM((2, tiles, ny, LANES), F32),
            pltpu.VMEM((2 * nl * nx, ny), F32),
            dma((3,)),
        ],
        compiler_params=pltpu.CompilerParams(vmem_limit_bytes=40 * 1024 * 1024),
        name="last_substep",
    )(*between)
    return wave.reshape(nx, ny, nk), cur.reshape(2, nl, nx, ny)


def solution(mesh):
    in_specs = (
        P("gx", "gy", "comp"),
        P("gx", "gy"),
        P(None, "comp"),
        P(),
        P(),
        P(None, "comp", "gx", "gy"),
        P("comp"),
    )
    out_specs = (P("gx", "gy", "comp"), P(None, "comp", "gx", "gy"))
    return jax.shard_map(local, mesh=mesh, in_specs=in_specs, out_specs=out_specs, check_vma=False)
```

```python
import functools

import jax
import jax.numpy as jnp
from jax import lax
from jax.experimental import pallas as pl
from jax.experimental.pallas import tpu as pltpu
from jax.sharding import PartitionSpec as P

SUBSTEPS = 3
DT = 0.5
VISC = 0.4
F32 = jnp.float32
BF16 = jnp.bfloat16
MESH = pl.DeviceIdType.MESH


PAD = 8
LANES = 128


BLOCK = 32


def advance(flow, stokes, mask_t, cor_t, drag, ny, i, firsts, store):
    block = BLOCK
    for first in firsts:
        at = PAD + first
        u, v = (flow[c, i + 1, at:at + block, :] for c in (0, 1))
        u_w, v_w = (flow[c, i, at:at + block, :] for c in (0, 1))
        u_e, v_e = (flow[c, i + 2, at:at + block, :] for c in (0, 1))
        u_s, v_s = (flow[c, i + 1, at - 1:at + block - 1, :] for c in (0, 1))
        u_n, v_n = (flow[c, i + 1, at + 1:at + block + 1, :] for c in (0, 1))
        rs = pl.ds(pl.multiple_of(i * ny + first, block), block)
        total = cor_t[first:first + block, :] + 0.5 * (v_e - v_w) - 0.5 * (u_n - u_s)
        lap_u = u_e + u_w + u_n + u_s - 4.0 * u
        lap_v = v_e + v_w + v_n + v_s - 4.0 * v
        m = mask_t[rs, :]
        u_new = m * (u + DT * (total * (v + stokes[rs, LANES:2 * LANES]) - drag * u + VISC * lap_u))
        v_new = m * (v + DT * (-total * (u + stokes[rs, 0:LANES]) - drag * v + VISC * lap_v))
        store(i, first, block, u_new, v_new)


def kernel(
    dims,
    spec_hbm, mask_hbm, cour_hbm, inter_hbm, proj_hbm, cur_hbm, drag_hbm,
    wave, last, stokes, mask_t, cor_t, drag_t,
    specx, adv, wmat, proj, projp, maskv, cour, curv, dragv,
    mask_b, fbuf, fbuf_n, ystage, ysend, yrecv, yhalo,
    flow, xsend, xrecv, vsend, vrecv,
    load_sem, hx_send, hx_recv, hy_send, hy_recv, av_send, av_recv,
    fx_send, fx_recv, fy_send, fy_recv,
):
    nx, ny, nk, nl = dims
    groups = LANES // nl
    tiles = nx // groups
    gx, gy, core = lax.axis_index("gx"), lax.axis_index("gy"), lax.axis_index("comp")
    n_gx, n_gy = lax.axis_size("gx"), lax.axis_size("gy")
    west = (lax.rem(gx + n_gx - 1, n_gx), gy, core)
    east = (lax.rem(gx + 1, n_gx), gy, core)
    south = (gx, lax.rem(gy + n_gy - 1, n_gy), core)
    north = (gx, lax.rem(gy + 1, n_gy), core)
    other = 1 - core
    partner = (gx, gy, other)
    not_first = jnp.where(gy > 0, 1.0, 0.0).astype(F32)
    not_last = jnp.where(gy < n_gy - 1, 1.0, 0.0).astype(F32)
    scope = jax.named_scope

    def rows(start, count):
        return pl.ds(pl.multiple_of(start * ny, ny), count * ny)

    with scope("t_sig"):
        barrier = pltpu.get_barrier_semaphore()
        for peer in (west, east, south, north, partner):
            pl.semaphore_signal(barrier, inc=1, device_id=peer, device_id_type=MESH)

    loads = []

    def load(src, dst):
        copy = pltpu.make_async_copy(src, dst, load_sem.at[len(loads)])
        copy.start()
        loads.append(copy)
        return copy

    def remote(src, dst, send, recv, peer):
        return pltpu.make_async_remote_copy(
            src_ref=src, dst_ref=dst, send_sem=send, recv_sem=recv,
            device_id=peer, device_id_type=MESH,
        )

    rim = 16
    rim_load = [
        load(spec_hbm.at[:, pl.ds(first, rim), :], specx.at[pl.ds(1, nx), pl.ds(first, rim), :])
        for first in (0, ny - rim)
    ]
    cur_load = load(cur_hbm, curv)
    mask_load = load(mask_hbm, maskv)
    cour_load = load(cour_hbm, cour)
    middle = pl.ds(rim, ny - 2 * rim)
    spec_load = load(spec_hbm.at[:, middle, :], specx.at[pl.ds(1, nx), middle, :])
    own_k = pl.ds(pl.multiple_of(core * nk, nk), nk)
    oth_k = pl.ds(pl.multiple_of(other * nk, nk), nk)
    own_l = pl.ds(pl.multiple_of(core * nl, nl), nl)
    proj_load = [
        load(proj_hbm.at[c, own_l, ks], proj.at[pl.ds(c * nl, nl), pl.ds(half * nk, nk)])
        for c in (0, 1) for half, ks in ((0, own_k), (1, oth_k))
    ]
    drag_load = load(drag_hbm, dragv)
    w_load = [
        load(inter_hbm.at[own_k, own_k], wmat.at[pl.ds(0, nk), :]),
        load(inter_hbm.at[oth_k, own_k], wmat.at[pl.ds(nk, nk), :]),
    ]
    with scope("t_spec"):
        for copy in rim_load:
            copy.wait()
    for x in range(nx):
        ystage[0, x:x + 1, :] = specx[1 + x, 0:rim, :].astype(F32)[0:1]
        ystage[1, x:x + 1, :] = specx[1 + x, ny - rim:ny, :].astype(F32)[rim - 1:rim]
    ysend[...] = ystage[...].astype(BF16)
    with scope("t_barrier"):
        pl.semaphore_wait(barrier, 5)
    hy = [
        remote(ysend.at[0], yrecv.at[1], hy_send.at[0], hy_recv.at[1], south),
        remote(ysend.at[1], yrecv.at[0], hy_send.at[1], hy_recv.at[0], north),
    ]
    for copy in hy:
        copy.start()
    def edge_of(n):
        return lax.rem(lax.rem(gx, 2) + n, 2)

    def hx(n):
        f = edge_of(n)
        peer = (lax.rem(gx + n_gx - 1 + 2 * f, n_gx), gy, core)
        return remote(
            spec_hbm.at[f * (nx - 1)], specx.at[(1 - f) * (nx + 1)],
            hx_send.at[n], hx_recv.at[n], peer,
        )

    for n in (0, 1):
        hx(n).start()

    inner = slice(PAD, PAD + ny)
    lane = lax.broadcasted_iota(jnp.int32, (ny, LANES), 1)
    half_lane = lax.broadcasted_iota(jnp.int32, (ny // 2, LANES), 1)
    half = ny // 2

    def state(s):
        return last if s == SUBSTEPS - 1 else flow.at[s]

    def flow_x(s):
        return [
            remote(xsend.at[s, 0], xrecv.at[s, 1], fx_send.at[s, 0], fx_recv.at[s, 1], west),
            remote(xsend.at[s, 1], xrecv.at[s, 0], fx_send.at[s, 1], fx_recv.at[s, 0], east),
        ]

    def flow_y(s):
        return [
            remote(vsend.at[s, 0], vrecv.at[s, 1], fy_send.at[s, 0], fy_recv.at[s, 1], south),
            remote(vsend.at[s, 1], vrecv.at[s, 0], fy_send.at[s, 1], fy_recv.at[s, 0], north),
        ]

    def turn(q, lanes):
        return pltpu.roll(q, lanes % LANES, 1) if lanes % LANES else q

    def send_flow_y(s):
        now = state(s)
        for c in (0, 1):
            for i in range(tiles):
                r = c * tiles + i
                vsend[s, 0, r:r + 1, :] = now[c, i + 1, PAD:PAD + 1, :]
                vsend[s, 1, r:r + 1, :] = now[c, i + 1, PAD + ny - 1:PAD + ny, :]
        for copy in flow_y(s):
            copy.start()

    def send_flow_x(s):
        now = state(s)
        for side, tile, group in ((0, 1, 0), (1, tiles, groups - 1)):
            packed = None
            for c in (0, 1):
                for h in (0, 1):
                    g = 2 * c + h
                    part = turn(now[c, tile, PAD + h * half:PAD + (h + 1) * half, :], nl * (g - group))
                    packed = part if packed is None else jnp.where(half_lane >= nl * g, part, packed)
            xsend[s, side] = packed.astype(BF16)
        for copy in flow_x(s):
            copy.start()

    def take_flow(s):
        now = state(s)
        for copy in flow_x(s):
            copy.wait_recv()
        for c in (0, 1):
            for h in (0, 1):
                g = 2 * c + h
                rs = slice(PAD + h * half, PAD + (h + 1) * half)
                from_west = turn(xrecv[s, 0].astype(F32), -nl * g)
                from_east = turn(xrecv[s, 1].astype(F32), nl * (groups - 1 - g))
                now[c, 0, rs, :] = jnp.where(half_lane < nl, from_west, turn(now[c, tiles, rs, :], nl))
                now[c, tiles + 1, rs, :] = jnp.where(
                    half_lane >= LANES - nl, from_east, turn(now[c, 1, rs, :], -nl)
                )
        for copy in flow_y(s):
            copy.wait_recv()
        for c in (0, 1):
            for i in range(tiles):
                r = c * tiles + i
                now[c, i + 1, PAD - 1:PAD, :] = vrecv[s, 0, r:r + 1, :] * not_first
                now[c, i + 1, PAD + ny:PAD + ny + 1, :] = vrecv[s, 1, r:r + 1, :] * not_last

    with scope("t_cur"):
        cur_load.wait()
    for c in (0, 1):
        for i in range(tiles):
            tile = jnp.concatenate(
                [curv[pl.ds(c * nl * nx + q * tiles + i, nl, stride=nx), :] for q in range(groups)], axis=0
            )
            flow[0, c, i + 1, inner, :] = tile.T
    send_flow_y(0)
    send_flow_x(0)

    mask_load.wait()
    cour_load.wait()
    turned = jnp.concatenate([maskv[...].astype(F32), jnp.zeros((ny - nx, ny), F32)], axis=0).T
    for x in range(nx):
        mask_b[x * ny:(x + 1) * ny, :] = jnp.broadcast_to(turned[:, x:x + 1], (ny, LANES))
    for i in range(tiles):
        mixed = mask_b[i * ny:(i + 1) * ny, :]
        for q in range(1, groups):
            x = q * tiles + i
            mixed = jnp.where(lane >= nl * q, mask_b[x * ny:(x + 1) * ny, :], mixed)
        mask_t[i * ny:(i + 1) * ny, :] = mixed

    lat = (gy * ny + lax.broadcasted_iota(jnp.int32, (ny, LANES), 0)).astype(F32)
    cor_t[...] = jnp.sin(jnp.pi * ((lat + 0.5) / (n_gy * ny) - 0.5))

    drag_load.wait()
    drag_t[...] = jnp.broadcast_to(jnp.concatenate([dragv[...]] * groups, axis=1), drag_t.shape)

    def finish_loads():
        for copy in w_load:
            copy.wait()

    for copy in proj_load:
        copy.wait()
    proj[2 * nl:LANES, :] = jnp.zeros((LANES - 2 * nl, 2 * nk), BF16)
    for q in range(groups):
        projp[q] = jnp.zeros(projp.shape[1:], BF16)
        for c in (0, 1):
            projp[q, c * LANES + q * nl:c * LANES + (q + 1) * nl, :] = proj[c * nl:(c + 1) * nl, :]

    chunks = nk // 128

    def swap(x, first, count, part):
        rs = pl.ds(pl.multiple_of(x * ny + first, rim), count)
        return remote(
            adv.at[rs, pl.ds(0, nk)], adv.at[rs, pl.ds(nk, nk)],
            av_send.at[part, x], av_recv.at[part, x], partner,
        )

    def swaps(x):
        return [swap(x, rim, ny - 2 * rim, 0), swap(x, 0, rim, 1), swap(x, ny - rim, rim, 2)]

    def advect(x, first, count, buf, base):
        rs = pl.ds(pl.multiple_of(x * ny + first, rim), count)
        mb = mask_b[rs, :]
        at = 8 + first - base
        for kc in range(chunks):
            ks = slice(kc * 128, (kc + 1) * 128)
            a, b = cour[0:1, ks], cour[1:2, ks]
            mag_a, mag_b = jnp.abs(a), jnp.abs(b)
            here = buf[kc, at:at + count, :]
            ys = slice(first, first + count)
            ux = jnp.where(a > 0, specx[x, ys, ks].astype(F32), specx[x + 2, ys, ks].astype(F32))
            uy = jnp.where(b > 0, buf[kc, at - 1:at + count - 1, :], buf[kc, at + 1:at + count + 1, :])
            new = (1.0 - mag_a - mag_b) * here + mag_a * ux + mag_b * uy
            adv[rs, ks] = (mb * new).astype(BF16)

    def widen(x, first, count, buf):
        for kc in range(chunks):
            ks = slice(kc * 128, (kc + 1) * 128)
            buf[kc, 8:8 + count, :] = specx[x + 1, first:first + count, ks].astype(F32)

    def halo_rows(x, side, row, buf):
        for kc in range(chunks):
            buf[kc, row:row + 1, :] = yhalo[side, kc, pl.ds(x, 1), :]

    def advect_middle(x, carry):
        widen(x, 0, ny, fbuf)
        advect(x, rim, ny - 2 * rim, fbuf, 0)
        swap(x, rim, ny - 2 * rim, 0).start()
        return carry

    def advect_rim(x, carry):
        widen(x, 0, 2 * rim, fbuf)
        halo_rows(x, 0, 7, fbuf)
        advect(x, 0, rim, fbuf, 0)
        swap(x, 0, rim, 1).start()
        widen(x, ny - 2 * rim, 2 * rim, fbuf_n)
        halo_rows(x, 1, 8 + 2 * rim, fbuf_n)
        advect(x, ny - rim, rim, fbuf_n, ny - 2 * rim)
        swap(x, ny - rim, rim, 2).start()
        return carry

    def advect_edge(n, carry):
        hx(n).wait_recv()
        x = edge_of(n) * (nx - 1)
        widen(x, 0, ny, fbuf)
        halo_rows(x, 0, 7, fbuf)
        halo_rows(x, 1, 8 + ny, fbuf)
        advect(x, 0, ny, fbuf, 0)
        swap(x, 0, ny, 0).start()
        return carry

    def drift(x, count, fresh):
        q, tile = x // tiles, x % tiles
        for each in range(x, x + count):
            for copy in swaps(each):
                copy.wait_recv()
        part = lax.dot_general(
            adv[rows(x, count), :], projp[q], (((1,), (1,)), ((), ())),
            preferred_element_type=F32,
        )
        rs = pl.ds(tile * ny, count * ny)
        stokes[rs, :] = part if fresh else stokes[rs, :] + part

    def drift_row(n, carry):
        f = edge_of(n)
        x, q, tile = f * (nx - 1), f * (groups - 1), f * (tiles - 1)
        swap(x, 0, ny, 0).wait_recv()
        part = lax.dot_general(
            adv[rows(x, 1), :], proj[...], (((1,), (1,)), ((), ())), preferred_element_type=F32,
        )
        mine = (lane >= q * nl) & (lane < (q + 1) * nl)
        rs = rows(tile, 1)
        for c in (0, 1):
            ls = slice(c * LANES, (c + 1) * LANES)
            moved = pltpu.roll(part, lax.rem(nl * q + LANES - nl * c, LANES), 1)
            stokes[rs, ls] = stokes[rs, ls] + jnp.where(mine, moved, 0.0)
        return carry

    drag_row = drag_t[0:1, :]

    def substep(s):
        now, then = state(s), state(s + 1)

        def store(i, first, block, u_new, v_new):
            at = slice(PAD + first, PAD + first + block)
            then[0, i + 1, at, :] = u_new
            then[1, i + 1, at, :] = v_new

        def some(firsts):
            def one(i, carry):
                advance(now, stokes, mask_t, cor_t, drag_row, ny, i, firsts, store)
                return carry

            lax.fori_loop(0, tiles, one, 0)

        some((0, ny - BLOCK))
        send_flow_y(s + 1)
        some(tuple(range(BLOCK, ny - BLOCK, BLOCK)))
        send_flow_x(s + 1)

    wide = 256

    def gain(p, carry):
        rs = rows(p * 4, 4)
        mb = mask_b[rs, :]
        mb = jnp.concatenate([mb] * (wide // 128), axis=1)
        for n in range(nk // wide):
            ns = slice(n * wide, (n + 1) * wide)
            got = jnp.dot(adv[rs, :], wmat[:, ns], preferred_element_type=F32)
            wave[rs, ns] = (mb * (adv[rs, ns].astype(F32) + got)).astype(BF16)
        return carry

    spec_load.wait()
    with scope("t_middle"):
        lax.fori_loop(1, nx - 1, advect_middle, 0)
    with scope("t_hy"):
        for copy in hy:
            copy.wait_recv()
    for kc in range(chunks):
        ks = slice(kc * 128, (kc + 1) * 128)
        yhalo[0, kc] = yrecv[0, :, ks].astype(F32) * not_first
        yhalo[1, kc] = yrecv[1, :, ks].astype(F32) * not_last
    with scope("t_rim"):
        lax.fori_loop(1, nx - 1, advect_rim, 0)
    with scope("t_late"):
        finish_loads()
    with scope("t_drift"):
        for q in range(1, groups - 1):
            drift(q * tiles, tiles, q == 1)
        drift(1, tiles - 1, False)
    with scope("t_hx"):
        lax.fori_loop(0, 2, advect_edge, 0)
    with scope("t_drift3"):
        drift(nx - tiles, tiles - 1, False)
    with scope("t_driftE"):
        lax.fori_loop(0, 2, drift_row, 0)
    with scope("t_take0"):
        take_flow(0)
    with scope("t_sub0"):
        substep(0)
    with scope("t_gainA"):
        lax.fori_loop(1, nx // 8 + 1, gain, 0)
    with scope("t_take1"):
        take_flow(1)
    with scope("t_sub1"):
        substep(1)
    with scope("t_gainB"):
        for p in [0] + list(range(nx // 8 + 1, nx // 4)):
            gain(p, 0)
    with scope("t_take2"):
        take_flow(2)

    with scope("t_out"):
        for copy in hy + [hx(0), hx(1)]:
            copy.wait_send()
        for s in range(SUBSTEPS):
            for copy in flow_x(s) + flow_y(s):
                copy.wait_send()

        def drain(x, carry):
            for copy in swaps(x):
                copy.wait_send()
            return carry

        lax.fori_loop(1, nx - 1, drain, 0)
        for x in (0, nx - 1):
            swap(x, 0, ny, 0).wait_send()


def finish(
    dims,
    wave, last, stokes, mask_t, cor_t, drag_t,
    wave_hbm, curo_hbm,
    done, coutv, out_sem,
):
    nx, ny, nk, nl = dims
    groups = LANES // nl
    tiles = nx // groups
    put = pltpu.make_async_copy(wave, wave_hbm, out_sem.at[0])
    put.start()
    drag_row = drag_t[0:1, :]

    def store(i, first, block, u_new, v_new):
        done[0, i, first:first + block, :] = u_new
        done[1, i, first:first + block, :] = v_new

    puts = [put]
    for i in range(tiles):
        advance(last, stokes, mask_t, cor_t, drag_row, ny, i, range(0, ny, BLOCK), store)
    for c in (0, 1):
        for i in range(tiles):
            tile = done[c, i].T
            for q in range(groups):
                coutv[pl.ds(c * nl * nx + q * tiles + i, nl, stride=nx), :] = tile[q * nl:(q + 1) * nl]
        part = pl.ds(c * nl * nx, nl * nx)
        put = pltpu.make_async_copy(coutv.at[part, :], curo_hbm.at[part, :], out_sem.at[1 + c])
        put.start()
        puts.append(put)
    for put in puts:
        put.wait()


def local(spectrum, sea_mask, courant, interaction, stokes_proj, currents, level_drag):
    nx, ny, nk = spectrum.shape
    nl = currents.shape[1]
    groups = LANES // nl
    tiles = nx // groups
    dims = (nx, ny, nk, nl)
    hbm = pl.BlockSpec(memory_space=pltpu.HBM)
    vmem = pl.BlockSpec(memory_space=pltpu.VMEM)
    dma = pltpu.SemaphoreType.DMA
    between = pl.pallas_call(
        functools.partial(kernel, dims),
        out_shape=(
            jax.ShapeDtypeStruct((nx * ny, nk), BF16),
            jax.ShapeDtypeStruct((2, tiles + 2, ny + 2 * PAD, LANES), F32),
            jax.ShapeDtypeStruct((tiles * ny, 2 * LANES), F32),
            jax.ShapeDtypeStruct((tiles * ny, LANES), F32),
            jax.ShapeDtypeStruct((ny, LANES), F32),
            jax.ShapeDtypeStruct((8, LANES), F32),
        ),
        in_specs=[hbm] * 7,
        out_specs=(vmem,) * 6,
        scratch_shapes=[
            pltpu.VMEM((nx + 2, ny, nk), BF16),
            pltpu.VMEM((nx * ny, 2 * nk), BF16),
            pltpu.VMEM((2 * nk, nk), BF16),
            pltpu.VMEM((LANES, 2 * nk), BF16),
            pltpu.VMEM((groups, 2 * LANES, 2 * nk), BF16),
            pltpu.VMEM((nx, ny), jnp.int32),
            pltpu.VMEM((2, nk), F32),
            pltpu.VMEM((2 * nl * nx, ny), F32),
            pltpu.VMEM((1, nl), F32),
            pltpu.VMEM((nx * ny, 128), F32),
            pltpu.VMEM((nk // 128, ny + 16, 128), F32),
            pltpu.VMEM((nk // 128, 48, 128), F32),
            pltpu.VMEM((2, nx, nk), F32),
            pltpu.VMEM((2, nx, nk), BF16),
            pltpu.VMEM((2, nx, nk), BF16),
            pltpu.VMEM((2, nk // 128, nx, 128), F32),
            pltpu.VMEM((SUBSTEPS - 1, 2, tiles + 2, ny + 2 * PAD, LANES), F32),
            pltpu.VMEM((SUBSTEPS, 2, ny // 2, LANES), BF16),
            pltpu.VMEM((SUBSTEPS, 2, ny // 2, LANES), BF16),
            pltpu.VMEM((SUBSTEPS, 2, 2 * tiles, LANES), F32),
            pltpu.VMEM((SUBSTEPS, 2, 2 * tiles, LANES), F32),
            dma((14,)),
            dma((2,)), dma((2,)), dma((2,)), dma((2,)),
            dma((3, nx)), dma((3, nx)),
            dma((SUBSTEPS, 2)), dma((SUBSTEPS, 2)), dma((SUBSTEPS, 2)), dma((SUBSTEPS, 2)),
        ],
        compiler_params=pltpu.CompilerParams(
            collective_id=0, has_side_effects=True, vmem_limit_bytes=40 * 1024 * 1024
        ),
        name="wave_ocean",
    )(*(pltpu.with_memory_space_constraint(each, pltpu.HBM) for each in (
        spectrum,
        sea_mask,
        courant,
        interaction,
        jnp.transpose(stokes_proj, (0, 2, 1)),
        currents.reshape(2 * nl * nx, ny),
        level_drag[None, :],
    )))
    wave, cur = pl.pallas_call(
        functools.partial(finish, dims),
        out_shape=(
            jax.ShapeDtypeStruct((nx * ny, nk), BF16),
            jax.ShapeDtypeStruct((2 * nl * nx, ny), F32),
        ),
        in_specs=[vmem] * 6,
        out_specs=(hbm, hbm),
        scratch_shapes=[
            pltpu.VMEM((2, tiles, ny, LANES), F32),
            pltpu.VMEM((2 * nl * nx, ny), F32),
            dma((3,)),
        ],
        compiler_params=pltpu.CompilerParams(vmem_limit_bytes=40 * 1024 * 1024),
        name="last_substep",
    )(*between)
    return wave.reshape(nx, ny, nk), cur.reshape(2, nl, nx, ny)


def solution(mesh):
    in_specs = (
        P("gx", "gy", "comp"),
        P("gx", "gy"),
        P(None, "comp"),
        P(),
        P(),
        P(None, "comp", "gx", "gy"),
        P("comp"),
    )
    out_specs = (P("gx", "gy", "comp"), P(None, "comp", "gx", "gy"))
    return jax.shard_map(local, mesh=mesh, in_specs=in_specs, out_specs=out_specs, check_vma=False)
```

```python
import functools

import jax
import jax.numpy as jnp
from jax import lax
from jax.experimental import pallas as pl
from jax.experimental.pallas import tpu as pltpu
from jax.sharding import PartitionSpec as P

SUBSTEPS = 3
DT = 0.5
VISC = 0.4
F32 = jnp.float32
BF16 = jnp.bfloat16
MESH = pl.DeviceIdType.MESH


PAD = 8
LANES = 128


BLOCK = 32


def advance(flow, stokes, mask_t, cor_t, drag, ny, i, firsts, store):
    block = BLOCK
    for first in firsts:
        at = PAD + first
        u, v = (flow[c, i + 1, at:at + block, :] for c in (0, 1))
        u_w, v_w = (flow[c, i, at:at + block, :] for c in (0, 1))
        u_e, v_e = (flow[c, i + 2, at:at + block, :] for c in (0, 1))
        u_s, v_s = (flow[c, i + 1, at - 1:at + block - 1, :] for c in (0, 1))
        u_n, v_n = (flow[c, i + 1, at + 1:at + block + 1, :] for c in (0, 1))
        rs = pl.ds(pl.multiple_of(i * ny + first, block), block)
        total = cor_t[first:first + block, :] + 0.5 * (v_e - v_w) - 0.5 * (u_n - u_s)
        lap_u = u_e + u_w + u_n + u_s - 4.0 * u
        lap_v = v_e + v_w + v_n + v_s - 4.0 * v
        m = mask_t[rs, :]
        u_new = m * (u + DT * (total * (v + stokes[rs, LANES:2 * LANES]) - drag * u + VISC * lap_u))
        v_new = m * (v + DT * (-total * (u + stokes[rs, 0:LANES]) - drag * v + VISC * lap_v))
        store(i, first, block, u_new, v_new)


def kernel(
    dims,
    spec_hbm, mask_hbm, cour_hbm, inter_hbm, proj_hbm, cur_hbm, drag_hbm,
    wave, last, stokes, mask_t, cor_t, drag_t,
    specx, adv, wmat, proj, projp, maskv, cour, curv, dragv,
    mask_b, fbuf, fbuf_n, ystage, ysend, yrecv, yhalo,
    flow, xsend, xrecv, vsend, vrecv,
    load_sem, hx_send, hx_recv, hy_send, hy_recv, av_send, av_recv,
    fx_send, fx_recv, fy_send, fy_recv,
):
    nx, ny, nk, nl = dims
    groups = LANES // nl
    tiles = nx // groups
    gx, gy, core = lax.axis_index("gx"), lax.axis_index("gy"), lax.axis_index("comp")
    n_gx, n_gy = lax.axis_size("gx"), lax.axis_size("gy")
    west = (lax.rem(gx + n_gx - 1, n_gx), gy, core)
    east = (lax.rem(gx + 1, n_gx), gy, core)
    south = (gx, lax.rem(gy + n_gy - 1, n_gy), core)
    north = (gx, lax.rem(gy + 1, n_gy), core)
    other = 1 - core
    partner = (gx, gy, other)
    not_first = jnp.where(gy > 0, 1.0, 0.0).astype(F32)
    not_last = jnp.where(gy < n_gy - 1, 1.0, 0.0).astype(F32)
    scope = jax.named_scope

    def rows(start, count):
        return pl.ds(pl.multiple_of(start * ny, ny), count * ny)

    with scope("t_sig"):
        barrier = pltpu.get_barrier_semaphore()
        for peer in (west, east, south, north, partner):
            pl.semaphore_signal(barrier, inc=1, device_id=peer, device_id_type=MESH)

    loads = []

    def load(src, dst):
        copy = pltpu.make_async_copy(src, dst, load_sem.at[len(loads)])
        copy.start()
        loads.append(copy)
        return copy

    def remote(src, dst, send, recv, peer):
        return pltpu.make_async_remote_copy(
            src_ref=src, dst_ref=dst, send_sem=send, recv_sem=recv,
            device_id=peer, device_id_type=MESH,
        )

    rim = 16
    rim_load = [
        load(spec_hbm.at[:, pl.ds(first, rim), :], specx.at[pl.ds(1, nx), pl.ds(first, rim), :])
        for first in (0, ny - rim)
    ]
    cur_load = load(cur_hbm, curv)
    mask_load = load(mask_hbm, maskv)
    cour_load = load(cour_hbm, cour)
    middle = pl.ds(rim, ny - 2 * rim)
    spec_load = load(spec_hbm.at[:, middle, :], specx.at[pl.ds(1, nx), middle, :])
    own_k = pl.ds(pl.multiple_of(core * nk, nk), nk)
    oth_k = pl.ds(pl.multiple_of(other * nk, nk), nk)
    own_l = pl.ds(pl.multiple_of(core * nl, nl), nl)
    proj_load = [
        load(proj_hbm.at[c, own_l, ks], proj.at[pl.ds(c * nl, nl), pl.ds(half * nk, nk)])
        for c in (0, 1) for half, ks in ((0, own_k), (1, oth_k))
    ]
    drag_load = load(drag_hbm, dragv)
    w_load = [
        load(inter_hbm.at[own_k, own_k], wmat.at[pl.ds(0, nk), :]),
        load(inter_hbm.at[oth_k, own_k], wmat.at[pl.ds(nk, nk), :]),
    ]
    with scope("t_spec"):
        for copy in rim_load:
            copy.wait()
    for x in range(nx):
        ystage[0, x:x + 1, :] = specx[1 + x, 0:rim, :].astype(F32)[0:1]
        ystage[1, x:x + 1, :] = specx[1 + x, ny - rim:ny, :].astype(F32)[rim - 1:rim]
    ysend[...] = ystage[...].astype(BF16)
    with scope("t_barrier"):
        pl.semaphore_wait(barrier, 5)
    hy = [
        remote(ysend.at[0], yrecv.at[1], hy_send.at[0], hy_recv.at[1], south),
        remote(ysend.at[1], yrecv.at[0], hy_send.at[1], hy_recv.at[0], north),
    ]
    for copy in hy:
        copy.start()
    def edge_of(n):
        return lax.rem(lax.rem(gx, 2) + n, 2)

    def hx(n):
        f = edge_of(n)
        peer = (lax.rem(gx + n_gx - 1 + 2 * f, n_gx), gy, core)
        return remote(
            spec_hbm.at[f * (nx - 1)], specx.at[(1 - f) * (nx + 1)],
            hx_send.at[n], hx_recv.at[n], peer,
        )

    for n in (0, 1):
        hx(n).start()

    inner = slice(PAD, PAD + ny)
    lane = lax.broadcasted_iota(jnp.int32, (ny, LANES), 1)
    half_lane = lax.broadcasted_iota(jnp.int32, (ny // 2, LANES), 1)
    half = ny // 2

    def state(s):
        return last if s == SUBSTEPS - 1 else flow.at[s]

    def flow_x(s):
        return [
            remote(xsend.at[s, 0], xrecv.at[s, 1], fx_send.at[s, 0], fx_recv.at[s, 1], west),
            remote(xsend.at[s, 1], xrecv.at[s, 0], fx_send.at[s, 1], fx_recv.at[s, 0], east),
        ]

    def flow_y(s):
        return [
            remote(vsend.at[s, 0], vrecv.at[s, 1], fy_send.at[s, 0], fy_recv.at[s, 1], south),
            remote(vsend.at[s, 1], vrecv.at[s, 0], fy_send.at[s, 1], fy_recv.at[s, 0], north),
        ]

    def turn(q, lanes):
        return pltpu.roll(q, lanes % LANES, 1) if lanes % LANES else q

    def send_flow_y(s):
        now = state(s)
        for c in (0, 1):
            for i in range(tiles):
                r = c * tiles + i
                vsend[s, 0, r:r + 1, :] = now[c, i + 1, PAD:PAD + 1, :]
                vsend[s, 1, r:r + 1, :] = now[c, i + 1, PAD + ny - 1:PAD + ny, :]
        for copy in flow_y(s):
            copy.start()

    def send_flow_x(s):
        now = state(s)
        for side, tile, group in ((0, 1, 0), (1, tiles, groups - 1)):
            packed = None
            for c in (0, 1):
                for h in (0, 1):
                    g = 2 * c + h
                    part = turn(now[c, tile, PAD + h * half:PAD + (h + 1) * half, :], nl * (g - group))
                    packed = part if packed is None else jnp.where(half_lane >= nl * g, part, packed)
            xsend[s, side] = packed.astype(BF16)
        for copy in flow_x(s):
            copy.start()

    def take_flow_x(s):
        now = state(s)
        for copy in flow_x(s):
            copy.wait_recv()
        for c in (0, 1):
            for h in (0, 1):
                g = 2 * c + h
                rs = slice(PAD + h * half, PAD + (h + 1) * half)
                from_west = turn(xrecv[s, 0].astype(F32), -nl * g)
                from_east = turn(xrecv[s, 1].astype(F32), nl * (groups - 1 - g))
                now[c, 0, rs, :] = jnp.where(half_lane < nl, from_west, turn(now[c, tiles, rs, :], nl))
                now[c, tiles + 1, rs, :] = jnp.where(
                    half_lane >= LANES - nl, from_east, turn(now[c, 1, rs, :], -nl)
                )

    def take_flow_y(s):
        now = state(s)
        for copy in flow_y(s):
            copy.wait_recv()
        for c in (0, 1):
            for i in range(tiles):
                r = c * tiles + i
                now[c, i + 1, PAD - 1:PAD, :] = vrecv[s, 0, r:r + 1, :] * not_first
                now[c, i + 1, PAD + ny:PAD + ny + 1, :] = vrecv[s, 1, r:r + 1, :] * not_last

    with scope("t_cur"):
        cur_load.wait()
    for c in (0, 1):
        for i in range(tiles):
            tile = jnp.concatenate(
                [curv[pl.ds(c * nl * nx + q * tiles + i, nl, stride=nx), :] for q in range(groups)], axis=0
            )
            flow[0, c, i + 1, inner, :] = tile.T
    send_flow_y(0)
    send_flow_x(0)

    mask_load.wait()
    cour_load.wait()
    turned = jnp.concatenate([maskv[...].astype(F32), jnp.zeros((ny - nx, ny), F32)], axis=0).T
    for x in range(nx):
        mask_b[x * ny:(x + 1) * ny, :] = jnp.broadcast_to(turned[:, x:x + 1], (ny, LANES))
    for i in range(tiles):
        mixed = mask_b[i * ny:(i + 1) * ny, :]
        for q in range(1, groups):
            x = q * tiles + i
            mixed = jnp.where(lane >= nl * q, mask_b[x * ny:(x + 1) * ny, :], mixed)
        mask_t[i * ny:(i + 1) * ny, :] = mixed

    lat = (gy * ny + lax.broadcasted_iota(jnp.int32, (ny, LANES), 0)).astype(F32)
    cor_t[...] = jnp.sin(jnp.pi * ((lat + 0.5) / (n_gy * ny) - 0.5))

    drag_load.wait()
    drag_t[...] = jnp.broadcast_to(jnp.concatenate([dragv[...]] * groups, axis=1), drag_t.shape)

    def finish_loads():
        for copy in w_load:
            copy.wait()

    for copy in proj_load:
        copy.wait()
    proj[2 * nl:LANES, :] = jnp.zeros((LANES - 2 * nl, 2 * nk), BF16)
    for q in range(groups):
        projp[q] = jnp.zeros(projp.shape[1:], BF16)
        for c in (0, 1):
            projp[q, c * LANES + q * nl:c * LANES + (q + 1) * nl, :] = proj[c * nl:(c + 1) * nl, :]

    chunks = nk // 128

    def swap(x, first, count, part):
        rs = pl.ds(pl.multiple_of(x * ny + first, rim), count)
        return remote(
            adv.at[rs, pl.ds(0, nk)], adv.at[rs, pl.ds(nk, nk)],
            av_send.at[part, x], av_recv.at[part, x], partner,
        )

    def swaps(x):
        return [swap(x, rim, ny - 2 * rim, 0), swap(x, 0, rim, 1), swap(x, ny - rim, rim, 2)]

    def advect(x, first, count, buf, base):
        rs = pl.ds(pl.multiple_of(x * ny + first, rim), count)
        mb = mask_b[rs, :]
        at = 8 + first - base
        for kc in range(chunks):
            ks = slice(kc * 128, (kc + 1) * 128)
            a, b = cour[0:1, ks], cour[1:2, ks]
            mag_a, mag_b = jnp.abs(a), jnp.abs(b)
            here = buf[kc, at:at + count, :]
            ys = slice(first, first + count)
            ux = jnp.where(a > 0, specx[x, ys, ks].astype(F32), specx[x + 2, ys, ks].astype(F32))
            uy = jnp.where(b > 0, buf[kc, at - 1:at + count - 1, :], buf[kc, at + 1:at + count + 1, :])
            new = (1.0 - mag_a - mag_b) * here + mag_a * ux + mag_b * uy
            adv[rs, ks] = (mb * new).astype(BF16)

    def widen(x, first, count, buf):
        for kc in range(chunks):
            ks = slice(kc * 128, (kc + 1) * 128)
            buf[kc, 8:8 + count, :] = specx[x + 1, first:first + count, ks].astype(F32)

    def halo_rows(x, side, row, buf):
        for kc in range(chunks):
            buf[kc, row:row + 1, :] = yhalo[side, kc, pl.ds(x, 1), :]

    def advect_middle(x, carry):
        widen(x, 0, ny, fbuf)
        advect(x, rim, ny - 2 * rim, fbuf, 0)
        swap(x, rim, ny - 2 * rim, 0).start()
        return carry

    def advect_rim(x, carry):
        widen(x, 0, 2 * rim, fbuf)
        halo_rows(x, 0, 7, fbuf)
        advect(x, 0, rim, fbuf, 0)
        swap(x, 0, rim, 1).start()
        widen(x, ny - 2 * rim, 2 * rim, fbuf_n)
        halo_rows(x, 1, 8 + 2 * rim, fbuf_n)
        advect(x, ny - rim, rim, fbuf_n, ny - 2 * rim)
        swap(x, ny - rim, rim, 2).start()
        return carry

    def advect_edge(n, carry):
        hx(n).wait_recv()
        x = edge_of(n) * (nx - 1)
        widen(x, 0, ny, fbuf)
        halo_rows(x, 0, 7, fbuf)
        halo_rows(x, 1, 8 + ny, fbuf)
        advect(x, 0, ny, fbuf, 0)
        swap(x, 0, ny, 0).start()
        return carry

    def drift(x, count, fresh):
        q, tile = x // tiles, x % tiles
        for each in range(x, x + count):
            for copy in swaps(each):
                copy.wait_recv()
        part = lax.dot_general(
            adv[rows(x, count), :], projp[q], (((1,), (1,)), ((), ())),
            preferred_element_type=F32,
        )
        rs = pl.ds(tile * ny, count * ny)
        stokes[rs, :] = part if fresh else stokes[rs, :] + part

    def drift_row(n, carry):
        f = edge_of(n)
        x, q, tile = f * (nx - 1), f * (groups - 1), f * (tiles - 1)
        swap(x, 0, ny, 0).wait_recv()
        part = lax.dot_general(
            adv[rows(x, 1), :], proj[...], (((1,), (1,)), ((), ())), preferred_element_type=F32,
        )
        mine = (lane >= q * nl) & (lane < (q + 1) * nl)
        rs = rows(tile, 1)
        for c in (0, 1):
            ls = slice(c * LANES, (c + 1) * LANES)
            moved = pltpu.roll(part, lax.rem(nl * q + LANES - nl * c, LANES), 1)
            stokes[rs, ls] = stokes[rs, ls] + jnp.where(mine, moved, 0.0)
        return carry

    drag_row = drag_t[0:1, :]

    def substep(s):
        now, then = state(s), state(s + 1)

        def store(i, first, block, u_new, v_new):
            at = slice(PAD + first, PAD + first + block)
            then[0, i + 1, at, :] = u_new
            then[1, i + 1, at, :] = v_new

        def some(count, tile, firsts):
            def one(n, carry):
                advance(now, stokes, mask_t, cor_t, drag_row, ny, tile(n), firsts, store)
                return carry

            lax.fori_loop(0, count, one, 0)

        return some

    edge_blocks = (0, ny - BLOCK)
    inner_blocks = tuple(range(BLOCK, ny - BLOCK, BLOCK))

    wide = 256

    def gain(p, carry):
        rs = rows(p * 4, 4)
        mb = mask_b[rs, :]
        mb = jnp.concatenate([mb] * (wide // 128), axis=1)
        for n in range(nk // wide):
            ns = slice(n * wide, (n + 1) * wide)
            got = jnp.dot(adv[rs, :], wmat[:, ns], preferred_element_type=F32)
            wave[rs, ns] = (mb * (adv[rs, ns].astype(F32) + got)).astype(BF16)
        return carry

    spec_load.wait()
    with scope("t_middle"):
        lax.fori_loop(1, nx - 1, advect_middle, 0)
    with scope("t_hy"):
        for copy in hy:
            copy.wait_recv()
    for kc in range(chunks):
        ks = slice(kc * 128, (kc + 1) * 128)
        yhalo[0, kc] = yrecv[0, :, ks].astype(F32) * not_first
        yhalo[1, kc] = yrecv[1, :, ks].astype(F32) * not_last
    with scope("t_rim"):
        lax.fori_loop(1, nx - 1, advect_rim, 0)
    with scope("t_late"):
        finish_loads()
    with scope("t_drift"):
        for q in range(1, groups - 1):
            drift(q * tiles, tiles, q == 1)
        drift(1, tiles - 1, False)
    with scope("t_hx"):
        lax.fori_loop(0, 2, advect_edge, 0)
    with scope("t_drift3"):
        drift(nx - tiles, tiles - 1, False)
    with scope("t_take0y"):
        take_flow_y(0)
    some = substep(0)
    with scope("t_sub0a"):
        some(tiles - 2, lambda n: n + 1, edge_blocks + inner_blocks)
    with scope("t_driftE"):
        lax.fori_loop(0, 2, drift_row, 0)
    with scope("t_take0x"):
        take_flow_x(0)
    with scope("t_sub0"):
        some(2, lambda n: n * (tiles - 1), edge_blocks)
        send_flow_y(1)
        some(2, lambda n: n * (tiles - 1), inner_blocks)
        send_flow_x(1)
    with scope("t_gainA"):
        lax.fori_loop(1, nx // 8 + 1, gain, 0)
    with scope("t_take1"):
        take_flow_x(1)
        take_flow_y(1)
    with scope("t_sub1"):
        some = substep(1)
        some(tiles, lambda n: n, edge_blocks)
        send_flow_y(2)
        some(tiles, lambda n: n, inner_blocks)
        send_flow_x(2)
    with scope("t_gainB"):
        for p in [0] + list(range(nx // 8 + 1, nx // 4)):
            gain(p, 0)
    with scope("t_take2"):
        take_flow_x(2)
        take_flow_y(2)

    with scope("t_out"):
        for copy in hy + [hx(0), hx(1)]:
            copy.wait_send()
        for s in range(SUBSTEPS):
            for copy in flow_x(s) + flow_y(s):
                copy.wait_send()

        def drain(x, carry):
            for copy in swaps(x):
                copy.wait_send()
            return carry

        lax.fori_loop(1, nx - 1, drain, 0)
        for x in (0, nx - 1):
            swap(x, 0, ny, 0).wait_send()


def finish(
    dims,
    wave, last, stokes, mask_t, cor_t, drag_t,
    wave_hbm, curo_hbm,
    done, coutv, out_sem,
):
    nx, ny, nk, nl = dims
    groups = LANES // nl
    tiles = nx // groups
    puts = []

    def put(src, dst):
        copy = pltpu.make_async_copy(src, dst, out_sem.at[len(puts)])
        copy.start()
        puts.append(copy)

    count = nx * ny // 4
    for n in range(4):
        part = pl.ds(n * count, count)
        put(wave.at[part, :], wave_hbm.at[part, :])
    drag_row = drag_t[0:1, :]

    def store(i, first, block, u_new, v_new):
        done[0, i, first:first + block, :] = u_new
        done[1, i, first:first + block, :] = v_new

    def one(i, carry):
        advance(last, stokes, mask_t, cor_t, drag_row, ny, i, range(0, ny, BLOCK), store)
        return carry

    lax.fori_loop(0, tiles, one, 0)
    for c in (0, 1):
        for i in range(tiles):
            tile = done[c, i].T
            for q in range(groups):
                coutv[pl.ds(c * nl * nx + q * tiles + i, nl, stride=nx), :] = tile[q * nl:(q + 1) * nl]
        part = pl.ds(c * nl * nx, nl * nx)
        put(coutv.at[part, :], curo_hbm.at[part, :])
    for copy in puts:
        copy.wait()


def local(spectrum, sea_mask, courant, interaction, stokes_proj, currents, level_drag):
    nx, ny, nk = spectrum.shape
    nl = currents.shape[1]
    groups = LANES // nl
    tiles = nx // groups
    dims = (nx, ny, nk, nl)
    hbm = pl.BlockSpec(memory_space=pltpu.HBM)
    vmem = pl.BlockSpec(memory_space=pltpu.VMEM)
    dma = pltpu.SemaphoreType.DMA
    between = pl.pallas_call(
        functools.partial(kernel, dims),
        out_shape=(
            jax.ShapeDtypeStruct((nx * ny, nk), BF16),
            jax.ShapeDtypeStruct((2, tiles + 2, ny + 2 * PAD, LANES), F32),
            jax.ShapeDtypeStruct((tiles * ny, 2 * LANES), F32),
            jax.ShapeDtypeStruct((tiles * ny, LANES), F32),
            jax.ShapeDtypeStruct((ny, LANES), F32),
            jax.ShapeDtypeStruct((8, LANES), F32),
        ),
        in_specs=[hbm] * 7,
        out_specs=(vmem,) * 6,
        scratch_shapes=[
            pltpu.VMEM((nx + 2, ny, nk), BF16),
            pltpu.VMEM((nx * ny, 2 * nk), BF16),
            pltpu.VMEM((2 * nk, nk), BF16),
            pltpu.VMEM((LANES, 2 * nk), BF16),
            pltpu.VMEM((groups, 2 * LANES, 2 * nk), BF16),
            pltpu.VMEM((nx, ny), jnp.int32),
            pltpu.VMEM((2, nk), F32),
            pltpu.VMEM((2 * nl * nx, ny), F32),
            pltpu.VMEM((1, nl), F32),
            pltpu.VMEM((nx * ny, 128), F32),
            pltpu.VMEM((nk // 128, ny + 16, 128), F32),
            pltpu.VMEM((nk // 128, 48, 128), F32),
            pltpu.VMEM((2, nx, nk), F32),
            pltpu.VMEM((2, nx, nk), BF16),
            pltpu.VMEM((2, nx, nk), BF16),
            pltpu.VMEM((2, nk // 128, nx, 128), F32),
            pltpu.VMEM((SUBSTEPS - 1, 2, tiles + 2, ny + 2 * PAD, LANES), F32),
            pltpu.VMEM((SUBSTEPS, 2, ny // 2, LANES), BF16),
            pltpu.VMEM((SUBSTEPS, 2, ny // 2, LANES), BF16),
            pltpu.VMEM((SUBSTEPS, 2, 2 * tiles, LANES), F32),
            pltpu.VMEM((SUBSTEPS, 2, 2 * tiles, LANES), F32),
            dma((14,)),
            dma((2,)), dma((2,)), dma((2,)), dma((2,)),
            dma((3, nx)), dma((3, nx)),
            dma((SUBSTEPS, 2)), dma((SUBSTEPS, 2)), dma((SUBSTEPS, 2)), dma((SUBSTEPS, 2)),
        ],
        compiler_params=pltpu.CompilerParams(
            collective_id=0, has_side_effects=True, vmem_limit_bytes=40 * 1024 * 1024
        ),
        name="wave_ocean",
    )(*(pltpu.with_memory_space_constraint(each, pltpu.HBM) for each in (
        spectrum,
        sea_mask,
        courant,
        interaction,
        jnp.transpose(stokes_proj, (0, 2, 1)),
        currents.reshape(2 * nl * nx, ny),
        level_drag[None, :],
    )))
    wave, cur = pl.pallas_call(
        functools.partial(finish, dims),
        out_shape=(
            jax.ShapeDtypeStruct((nx * ny, nk), BF16),
            jax.ShapeDtypeStruct((2 * nl * nx, ny), F32),
        ),
        in_specs=[vmem] * 6,
        out_specs=(hbm, hbm),
        scratch_shapes=[
            pltpu.VMEM((2, tiles, ny, LANES), F32),
            pltpu.VMEM((2 * nl * nx, ny), F32),
            dma((6,)),
        ],
        compiler_params=pltpu.CompilerParams(vmem_limit_bytes=40 * 1024 * 1024),
        name="last_substep",
    )(*between)
    return wave.reshape(nx, ny, nk), cur.reshape(2, nl, nx, ny)


def solution(mesh):
    in_specs = (
        P("gx", "gy", "comp"),
        P("gx", "gy"),
        P(None, "comp"),
        P(),
        P(),
        P(None, "comp", "gx", "gy"),
        P("comp"),
    )
    out_specs = (P("gx", "gy", "comp"), P(None, "comp", "gx", "gy"))
    return jax.shard_map(local, mesh=mesh, in_specs=in_specs, out_specs=out_specs, check_vma=False)
```
